32 devices in a mesh: batch: 2 (over x), ctx: 8 (over z, y), mp: 2 (over core).
Axes of the slice: x: 2, y: 2, z: 4, core: 2. Of those that a mesh axis runs over, the one named last changes fastest.
Arguments:
- tokens: bfloat16 [4, 1024, 1600], P(('batch', 'mp'), 'ctx'), may hold values from -6 to 6
- cotangent: bfloat16 [4, 1024, 1600], P(('batch', 'mp'), 'ctx'), may hold values from -6 to 6
- block_table: int32 [16], replicated, may hold values from 0 to 15, each once
- w_qkv: bfloat16 [1600, 4800], replicated, may hold values from -6 to 6
- q_bias: float32 [1600], replicated, may hold values from -3 to 3
- v_bias: float32 [1600], replicated, may hold values from -3 to 3
- w_out: bfloat16 [1600, 1600], replicated, may hold values from -2.5 to 2.5
- out_bias: float32 [1600], replicated, may hold values from -3 to 3
- ln1_gain: float32 [1600], replicated, may hold values from 0.5 to 1.5
- ln1_bias: float32 [1600], replicated, may hold values from -3 to 3
- ln2_gain: float32 [1600], replicated, may hold values from 0.5 to 1.5
- ln2_bias: float32 [1600], replicated, may hold values from -3 to 3
- w_up: bfloat16 [1600, 6400], P(None, 'mp'), may hold values from -0.15625 to 0.15625
- up_bias: float32 [6400], P('mp'), may hold values from -3 to 3
- w_down: bfloat16 [6400, 1600], P('mp'), may hold values from -0.078125 to 0.078125
- down_bias: float32 [1600], replicated, may hold values from -3 to 3
Outputs:
- layer_out: bfloat16 [4, 1024, 1600], P(('batch', 'mp'), 'ctx')
- tokens_grad: bfloat16 [4, 1024, 1600], P(('batch', 'mp'), 'ctx')
- w_qkv_grad: float32 [1600, 4800], P(('batch', 'ctx'), 'mp')
- w_out_grad: float32 [1600, 1600], P(('batch', 'ctx'), 'mp')
- w_up_grad: float32 [1600, 6400], P(('batch', 'ctx'), 'mp')
- w_down_grad: float32 [6400, 1600], P('mp', ('batch', 'ctx'))
- up_bias_grad: float32 [6400], P('mp')
- vector_grads: float32 [8, 1600], replicated
The draws below stay inside these ranges and needn't reach their ends.
Inputs may be any that keep to these rules, and one draw needn't show every extreme that they name: `block_table`: each number appears once.
All inputs are finite; a program needn't handle non-finite values.
Results may differ from the reference program's by a relative error of at most 0.015.
Values may be sent and summed in bfloat16 or wider, within the bound.
No kernel may reach another device: no remote copies, remote signals or barrier semaphores. Data moves between devices by JAX's collectives and lax.ppermute only.
A program may use at most 448 MiB of HBM per device.

```python
import math
import jax
import jax.numpy as jnp
from jax import lax

D = 1600
H = 25
HD = 64
FF = 6400
ROWS = 128
BLK = 64
NBLK = 16
LEN = 1024
SEQS = 4
N_CTX = 8


def draw_w_qkv(key, part):
    base_key = jax.random.fold_in(key, 0)
    base_draw = jnp.clip(jax.random.normal(base_key, (D, 3 * D), jnp.float32), -6.0, 6.0)
    base_draw = base_draw * (1.0 / math.sqrt(D))
    return base_draw.astype(jnp.bfloat16)


def level_of(own_key, extent, shards, smallest, top_value):
    gain, own = 1.0, jax.random.fold_in(own_key, 6)
    for dim, blocks in shards:
        steps = jnp.exp(jax.random.uniform(jax.random.fold_in(own, dim), (blocks,), jnp.float32, smallest / len(shards), top_value / len(shards)))
        gain = gain * jnp.repeat(steps, extent[dim] // blocks).reshape([-1 if axis == dim else 1 for axis in range(len(extent))])
    return gain


def centred(rng, shape, scale, bound, shards=(), kind=jnp.bfloat16):
    gain = level_of(rng, shape, shards, -0.22, 0.18) if shards else 1.0
    array = jax.random.normal(rng, shape, jnp.float32) * scale * gain
    return jnp.minimum(jnp.maximum(array, -bound), bound).astype(kind)


def setup_inputs(seed: int = 0) -> dict:
    streams_of = jax.random.split(jax.random.key(seed), 17)
    tokens = centred(streams_of[0], (SEQS, LEN, D), 1.0, 6.0, ((0, 4), (1, 8)))
    cotangent = centred(streams_of[1], (SEQS, LEN, D), 1.0, 6.0, ((0, 4), (1, 8)))
    block_table = jax.random.permutation(streams_of[2], NBLK).astype(jnp.int32)
    w_qkv = draw_w_qkv(jax.random.fold_in(streams_of[16], 71), 0)
    q_bias = centred(streams_of[4], (D,), 0.5, 3.0, (), jnp.float32)
    v_bias = centred(streams_of[5], (D,), 0.5, 3.0, (), jnp.float32)
    w_out = centred(streams_of[6], (D, D), (max(1, 4 * D // LEN)) ** -0.5, 2.5)
    out_bias = centred(streams_of[7], (D,), 0.5, 3.0, (), jnp.float32)
    ln1_gain = jnp.clip(1.0 + 0.1 * jax.random.normal(streams_of[8], (D,), jnp.float32), 0.5, 1.5)
    ln1_bias = centred(streams_of[9], (D,), 0.5, 3.0, (), jnp.float32)
    ln2_gain = jnp.clip(1.0 + 0.1 * jax.random.normal(streams_of[10], (D,), jnp.float32), 0.5, 1.5)
    ln2_bias = centred(streams_of[11], (D,), 0.5, 3.0, (), jnp.float32)
    w_up = centred(streams_of[12], (D, FF), D ** -0.5, 0.15625, ((1, 2),))
    up_bias = centred(streams_of[13], (FF,), 0.5, 3.0, ((0, 2),), jnp.float32)
    w_down = centred(streams_of[14], (FF, D), FF ** -0.5, 0.078125, ((0, 2),))
    down_bias = centred(streams_of[15], (D,), 0.5, 3.0, (), jnp.float32)
    return {"tokens": tokens, "cotangent": cotangent, "block_table": block_table, "w_qkv": w_qkv, "q_bias": q_bias, "v_bias": v_bias, "w_out": w_out, "out_bias": out_bias, "ln1_gain": ln1_gain, "ln1_bias": ln1_bias, "ln2_gain": ln2_gain, "ln2_bias": ln2_bias, "w_up": w_up, "up_bias": up_bias, "w_down": w_down, "down_bias": down_bias}


NORM_EPSILON = 1e-05
MASKED_SCORE = -1e+30

def layer_norm(row_values, row_gain, row_shift):
    row_mean = lax.optimization_barrier(jnp.mean(row_values, axis=-1, keepdims=True))
    centered = row_values - row_mean
    row_var = lax.optimization_barrier(jnp.mean(centered * centered, axis=-1, keepdims=True))
    return centered * lax.rsqrt(row_var + NORM_EPSILON) * row_gain + row_shift

def gelu_tanh(values):
    return jax.nn.gelu(values, approximate=True)

def positions_of(block_table):
    offsets = jnp.arange(BLK, dtype=jnp.int32)
    return (block_table[:, None] * BLK + offsets[None, :]).reshape(-1).astype(jnp.int32)

def round_low(values):
    return lax.optimization_barrier(values.astype(jnp.bfloat16)).astype(jnp.float32)

def reference(tokens, cotangent, block_table, w_qkv, q_bias, v_bias, w_out, out_bias, ln1_gain, ln1_bias, ln2_gain, ln2_bias, w_up, up_bias, w_down, down_bias):
    positions = positions_of(block_table)
    score_scale = HD ** (-0.5)
    qkv_shift = jnp.concatenate([q_bias, jnp.zeros((D,), jnp.float32), v_bias])
    block_ids = jnp.arange(N_CTX, dtype=jnp.int32)

    def one_sequence(totals, inputs):
        seq_tokens, seq_cot = inputs
        resid_in = seq_tokens.astype(jnp.float32)
        normed_one = layer_norm(resid_in, ln1_gain, ln1_bias).astype(jnp.bfloat16)
        qkv_rows = (jnp.dot(normed_one, w_qkv, preferred_element_type=jnp.float32) + qkv_shift).astype(jnp.bfloat16)
        query_all = qkv_rows[:, :D].reshape(LEN, H, HD).astype(jnp.float32)
        key_all = qkv_rows[:, D:2 * D].reshape(LEN, H, HD).astype(jnp.float32)
        value_all = qkv_rows[:, 2 * D:].reshape(LEN, H, HD).astype(jnp.float32)

        def block_scores(block_id):
            first_row = (block_id * ROWS).astype(jnp.int32)
            query_blk = lax.dynamic_slice_in_dim(query_all, first_row, ROWS, 0)
            query_pos = lax.dynamic_slice_in_dim(positions, first_row, ROWS, 0)
            raw = jnp.einsum('qhd,khd->hqk', query_blk, key_all) * score_scale
            allowed = positions[None, None, :] <= query_pos[None, :, None]
            return (query_blk, jnp.where(allowed, raw, MASKED_SCORE), allowed)

        def forward_block(block_id):
            query_blk, scores, allowed = block_scores(block_id)
            row_top = lax.optimization_barrier(jnp.max(scores, axis=-1))
            log_total = row_top + jnp.log(lax.optimization_barrier(jnp.sum(jnp.exp(scores - row_top[:, :, None]), axis=-1)))
            weights = round_low(jnp.where(allowed, jnp.exp(scores - log_total[:, :, None]), 0.0))
            attended = jnp.einsum('hqk,khd->qhd', weights, value_all)
            return (attended.reshape(ROWS, D).astype(jnp.bfloat16), log_total)
        attn_blocks, log_totals = lax.map(forward_block, block_ids)
        attn_rows = attn_blocks.reshape(LEN, D)
        resid_mid = resid_in + jnp.dot(attn_rows, w_out, preferred_element_type=jnp.float32) + out_bias
        normed_two = layer_norm(resid_mid, ln2_gain, ln2_bias).astype(jnp.bfloat16)
        pre_act = jnp.dot(normed_two, w_up, preferred_element_type=jnp.float32) + up_bias
        hidden = gelu_tanh(pre_act).astype(jnp.bfloat16)
        layer_rows = resid_mid + jnp.dot(hidden, w_down, preferred_element_type=jnp.float32) + down_bias
        cot_full = seq_cot.astype(jnp.float32)
        grad_hidden = jnp.dot(seq_cot, w_down.T, preferred_element_type=jnp.float32)
        unused, gelu_back = jax.vjp(gelu_tanh, pre_act)
        grad_pre = gelu_back(grad_hidden)[0]
        grad_pre_low = grad_pre.astype(jnp.bfloat16)
        down_grad = jnp.dot(hidden.T, seq_cot, preferred_element_type=jnp.float32)
        up_grad = jnp.dot(normed_two.T, grad_pre_low, preferred_element_type=jnp.float32)
        up_shift_grad = lax.optimization_barrier(jnp.sum(grad_pre, axis=0))
        grad_normed_two = jnp.dot(grad_pre_low, w_up.T, preferred_element_type=jnp.float32)
        unused, norm_two_back = jax.vjp(layer_norm, resid_mid, ln2_gain, ln2_bias)
        mid_part, gain_two_grad, shift_two_grad = norm_two_back(grad_normed_two)
        grad_mid = cot_full + mid_part
        grad_mid_low = grad_mid.astype(jnp.bfloat16)
        out_grad = jnp.dot(attn_rows.T, grad_mid_low, preferred_element_type=jnp.float32)
        grad_attn = jnp.dot(grad_mid_low, w_out.T, preferred_element_type=jnp.float32).astype(jnp.bfloat16)
        grad_attn_heads = grad_attn.reshape(LEN, H, HD).astype(jnp.float32)
        delta = lax.optimization_barrier(jnp.sum(grad_attn_heads * attn_rows.reshape(LEN, H, HD).astype(jnp.float32), axis=-1))

        def backward_block(kv_sum, block_id):
            query_blk, scores, allowed = block_scores(block_id)
            first_row = (block_id * ROWS).astype(jnp.int32)
            grad_blk = lax.dynamic_slice_in_dim(grad_attn_heads, first_row, ROWS, 0)
            delta_blk = lax.dynamic_slice_in_dim(delta, first_row, ROWS, 0)
            log_total = lax.dynamic_index_in_dim(log_totals, block_id, 0, keepdims=False)
            probs = jnp.where(allowed, jnp.exp(scores - log_total[:, :, None]), 0.0)
            grad_probs = jnp.einsum('qhd,khd->hqk', grad_blk, value_all)
            grad_scores = round_low(probs * (grad_probs - delta_blk.T[:, :, None]))
            probs_low = round_low(probs)
            grad_query = jnp.einsum('hqk,khd->qhd', grad_scores, key_all) * score_scale
            grad_key = jnp.einsum('hqk,qhd->khd', grad_scores, query_blk) * score_scale
            grad_value = jnp.einsum('hqk,qhd->khd', probs_low, grad_blk)
            term = round_low(jnp.concatenate([grad_key.reshape(LEN, D), grad_value.reshape(LEN, D)], axis=1))
            return (kv_sum + term, grad_query.reshape(ROWS, D))
        grad_kv, query_blocks = lax.scan(backward_block, jnp.zeros((LEN, 2 * D), jnp.float32), block_ids)
        grad_query_all = query_blocks.reshape(LEN, D)
        grad_qkv_low = jnp.concatenate([grad_query_all, grad_kv], axis=1).astype(jnp.bfloat16)
        qkv_grad = jnp.dot(normed_one.T, grad_qkv_low, preferred_element_type=jnp.float32)
        grad_normed_one = jnp.dot(grad_qkv_low, w_qkv.T, preferred_element_type=jnp.float32)
        unused, norm_one_back = jax.vjp(layer_norm, resid_in, ln1_gain, ln1_bias)
        in_part, gain_one_grad, shift_one_grad = norm_one_back(grad_normed_one)
        tokens_grad_rows = (grad_mid + in_part).astype(jnp.bfloat16)
        vectors = jnp.stack([gain_one_grad, shift_one_grad, lax.optimization_barrier(jnp.sum(grad_query_all, axis=0)), lax.optimization_barrier(jnp.sum(grad_kv[:, D:], axis=0)), lax.optimization_barrier(jnp.sum(grad_mid, axis=0)), gain_two_grad, shift_two_grad, lax.optimization_barrier(jnp.sum(cot_full, axis=0))])
        new_totals = (totals[0] + qkv_grad, totals[1] + out_grad, totals[2] + up_grad, totals[3] + down_grad, totals[4] + up_shift_grad, totals[5] + vectors)
        return (new_totals, (layer_rows.astype(jnp.bfloat16), tokens_grad_rows))
    start_totals = (jnp.zeros((D, 3 * D), jnp.float32), jnp.zeros((D, D), jnp.float32), jnp.zeros((D, FF), jnp.float32), jnp.zeros((FF, D), jnp.float32), jnp.zeros((FF,), jnp.float32), jnp.zeros((8, D), jnp.float32))
    totals, outputs = lax.scan(one_sequence, start_totals, (tokens, cotangent))
    return (outputs[0], outputs[1], totals[0], totals[1], totals[2], totals[3], totals[4], totals[5])
```

```python
import functools

import jax
import jax.numpy as jnp
from jax import lax
from jax.experimental import pallas as pl
from jax.experimental.pallas import tpu as pltpu
from jax.sharding import PartitionSpec as P

HD = 64
NORM_EPSILON = 1e-05
MASKED_SCORE = -1e30
GELU_C = 0.7978845608028654
GELU_A = 0.044715
LOW = jnp.bfloat16
F32 = jnp.float32


def norm_parts(rows):
    mean = jnp.mean(rows, axis=-1, keepdims=True)
    centered = rows - mean
    var = jnp.mean(centered * centered, axis=-1, keepdims=True)
    rstd = lax.rsqrt(var + NORM_EPSILON)
    return centered * rstd, rstd


def norm_back(grad, xhat, rstd, gain):
    scaled = grad * gain
    mean_one = jnp.mean(scaled, axis=-1, keepdims=True)
    mean_two = jnp.mean(scaled * xhat, axis=-1, keepdims=True)
    rows = rstd * (scaled - mean_one - xhat * mean_two)
    return rows, jnp.sum(grad * xhat, axis=0), jnp.sum(grad, axis=0)


def dot(left, right, dims):
    return lax.dot_general(left, right, (dims, ((), ())), preferred_element_type=F32)


def flip(value, axis, bit=1):
    size = lax.axis_size(axis)
    return lax.ppermute(value, axis, [(i, i ^ bit) for i in range(size)])


def ring_of(size):
    evens = list(range(0, size, 2))
    odds = list(range(1, size, 2))
    return evens + odds[::-1]


def shift(value, ring, step):
    size = len(ring)
    return lax.ppermute(value, "ctx", [(ring[i], ring[(i + step) % size]) for i in range(size)])


def ring_gather(own, ring):
    size = len(ring)
    half = size // 2
    ahead, behind = own, own
    blocks = [None] * size
    blocks[0] = own
    for step in range(1, half):
        ahead = shift(ahead, ring, 1)
        behind = shift(behind, ring, -1)
        blocks[step] = ahead
        blocks[size - step] = behind
    cut = own.shape[0] // 2
    last = jnp.concatenate([shift(ahead[:cut], ring, 1), shift(behind[cut:], ring, -1)], axis=0)
    blocks[half] = last
    return jnp.concatenate(blocks, axis=0)


def lanes_of(shape, axis, head):
    lane = lax.broadcasted_iota(jnp.int32, shape, axis)
    return (lane >= head * HD) & (lane < (head + 1) * HD)


def attn_forward_kernel(heads, q_ref, k_ref, v_ref, kpos_ref, qpos_ref, o_ref, lse_ref):
    keys = k_ref[...]
    values = v_ref[...]
    queries = q_ref[...] * LOW(HD**-0.5)
    allowed = kpos_ref[...] <= qpos_ref[0]
    total = None
    for head in range(heads):
        part = jnp.where(lanes_of(queries.shape, 1, head), queries, LOW(0))
        scores = dot(keys, part, ((1,), (1,)))
        scores = jnp.where(allowed, scores, MASKED_SCORE)
        top = jnp.max(scores, axis=0, keepdims=True)
        weights = jnp.exp(scores - top)
        mass = jnp.sum(weights, axis=0, keepdims=True)
        lse_ref[0, 0, head : head + 1, :] = top + jnp.log(mass)
        out = dot(values, weights.astype(LOW), ((0,), (0,))) * (1.0 / mass)
        total = out if head == 0 else jnp.where(lanes_of(out.shape, 0, head), out, total)
    o_ref[...] = total.T.astype(LOW)


def attn_backward_kernel(
    heads, tiles, q_ref, k_ref, v_ref, g_ref, o_ref, lse_ref, kpos_ref, qpos_ref,
    dq_ref, dk_ref, dv_ref, k_acc, v_acc,
):
    tile = pl.program_id(1)
    keys = k_ref[...]
    values = v_ref[...]
    queries = q_ref[...] * LOW(HD**-0.5)
    grads = g_ref[...]
    allowed = kpos_ref[...] <= qpos_ref[0]
    product = (grads.astype(F32) * o_ref[...].astype(F32)).T

    @pl.when(tile == 0)
    def _():
        k_acc[...] = jnp.zeros_like(k_acc)
        v_acc[...] = jnp.zeros_like(v_acc)

    total = None
    for head in range(heads):
        pick = lanes_of(queries.shape, 1, head)
        part = jnp.where(pick, queries, LOW(0))
        grad = jnp.where(pick, grads, LOW(0))
        delta = jnp.sum(product[head * HD : (head + 1) * HD, :], axis=0, keepdims=True)
        scores = dot(keys, part, ((1,), (1,)))
        probs = jnp.where(allowed, jnp.exp(scores - lse_ref[0, 0, head : head + 1, :]), 0.0)
        back = dot(values, grad, ((1,), (1,)))
        inner = (probs * (back - delta)).astype(LOW)
        v_acc[...] += dot(probs.astype(LOW), grad, ((1,), (0,)))
        k_acc[...] += dot(inner, part, ((1,), (0,)))
        out = dot(keys, inner, ((0,), (0,)))
        total = out if head == 0 else jnp.where(lanes_of(out.shape, 0, head), out, total)
    dq_ref[...] = (total * (HD**-0.5)).T.astype(LOW)

    @pl.when(tile == tiles - 1)
    def _():
        dk_ref[...] = k_acc[...].astype(LOW)
        dv_ref[...] = v_acc[...].astype(LOW)


def attn_sizes(rows, width):
    heads = 2 if (width // HD) % 2 == 0 else 1
    block = heads * HD
    tile = min(256, rows)
    return heads, block, width // block, tile, rows // tile


def qkv_views(qkv):
    rows, width = qkv.shape[0], qkv.shape[1] // 3
    heads, block, groups, tile, tiles = attn_sizes(rows, width)
    if block % 128 == 0:
        args = [qkv] * 3
        offsets = [0, groups, 2 * groups]
    else:
        args = [qkv[:, i * width : (i + 1) * width] for i in range(3)]
        offsets = [0, 0, 0]
    return args, [
        pl.BlockSpec((tile, block), lambda g, t: (t, g)),
        pl.BlockSpec((rows, block), lambda g, t: (0, offsets[1] + g)),
        pl.BlockSpec((rows, block), lambda g, t: (0, offsets[2] + g)),
    ]


def attn_forward(qkv, key_pos, query_pos):
    rows, width = qkv.shape[0], qkv.shape[1] // 3
    heads, block, groups, tile, tiles = attn_sizes(rows, width)
    qkv_args, qkv_specs = qkv_views(qkv)
    return pl.pallas_call(
        functools.partial(attn_forward_kernel, heads),
        grid=(groups, tiles),
        in_specs=[
            *qkv_specs,
            pl.BlockSpec((rows, 1), lambda g, t: (0, 0)),
            pl.BlockSpec((1, 1, tile), lambda g, t: (t, 0, 0)),
        ],
        out_specs=[
            pl.BlockSpec((tile, block), lambda g, t: (t, g)),
            pl.BlockSpec((1, 1, heads, tile), lambda g, t: (g, t, 0, 0)),
        ],
        out_shape=[
            jax.ShapeDtypeStruct((rows, width), LOW),
            jax.ShapeDtypeStruct((groups, tiles, heads, tile), F32),
        ],
        compiler_params=pltpu.CompilerParams(vmem_limit_bytes=60 << 20),
        cost_estimate=pl.CostEstimate(
            flops=4 * rows * rows * width, transcendentals=rows * rows * width // HD, bytes_accessed=8 * rows * width
        ),
        name="attn_forward",
    )(*qkv_args, key_pos, query_pos)


def attn_backward(qkv, grads, outs, lse, key_pos, query_pos):
    rows, width = qkv.shape[0], qkv.shape[1] // 3
    heads, block, groups, tile, tiles = attn_sizes(rows, width)
    qkv_args, qkv_specs = qkv_views(qkv)
    whole = pl.BlockSpec((rows, block), lambda g, t: (0, g))
    tiled = pl.BlockSpec((tile, block), lambda g, t: (t, g))
    return pl.pallas_call(
        functools.partial(attn_backward_kernel, heads, tiles),
        grid=(groups, tiles),
        in_specs=[
            *qkv_specs,
            tiled,
            tiled,
            pl.BlockSpec((1, 1, heads, tile), lambda g, t: (g, t, 0, 0)),
            pl.BlockSpec((rows, 1), lambda g, t: (0, 0)),
            pl.BlockSpec((1, 1, tile), lambda g, t: (t, 0, 0)),
        ],
        out_specs=[tiled, whole, whole],
        out_shape=[jax.ShapeDtypeStruct((rows, width), LOW)] * 3,
        scratch_shapes=[pltpu.VMEM((rows, block), F32), pltpu.VMEM((rows, block), F32)],
        compiler_params=pltpu.CompilerParams(vmem_limit_bytes=60 << 20),
        cost_estimate=pl.CostEstimate(
            flops=10 * rows * rows * width, transcendentals=rows * rows * width // HD, bytes_accessed=16 * rows * width
        ),
        name="attn_backward",
    )(*qkv_args, grads, outs, lse, key_pos, query_pos)


def shards(
    tokens, cotangent, block_table, w_qkv, q_bias, v_bias, w_out, out_bias,
    ln1_gain, ln1_bias, ln2_gain, ln2_bias, w_up, up_bias, w_down, down_bias,
):
    n_ctx, n_mp, n_batch = lax.axis_size("ctx"), lax.axis_size("mp"), lax.axis_size("batch")
    ctx, mp, batch = lax.axis_index("ctx"), lax.axis_index("mp"), lax.axis_index("batch")
    rows, dim = tokens.shape[1], tokens.shape[2]
    total = rows * n_ctx
    blk = total // block_table.shape[0]
    n_heads = dim // HD
    per = -(-n_heads // n_ctx)
    width = per * HD
    hid_half = w_up.shape[1]
    hid = hid_half // n_batch
    part = dim // (n_batch * n_ctx)

    ring = ring_of(n_ctx)
    place = [ring.index(i) for i in range(n_ctx)]
    ring_arr = jnp.array(ring, jnp.int32)
    at = jnp.array(place, jnp.int32)[ctx]
    steps = jnp.arange(n_ctx, dtype=jnp.int32)
    sources = ring_arr[(at - steps) % n_ctx]
    groups = ring_arr[(at + steps) % n_ctx]

    def first_head(group):
        return min(group * per, n_heads - per)

    blocks_per = rows // blk
    pos_ids = (sources[:, None] * blocks_per + jnp.arange(blocks_per, dtype=jnp.int32)[None, :]).reshape(-1)
    pos = (block_table[pos_ids][:, None] * blk + jnp.arange(blk, dtype=jnp.int32)[None, :]).reshape(-1)
    key_pos = pos[:, None]
    query_pos = pos.reshape(-1, 1, min(256, total))

    head_start = jnp.minimum(ctx * per, n_heads - per) * HD
    w_own = jnp.concatenate(
        [lax.dynamic_slice(w_qkv, (0, head_start + i * dim), (dim, width)) for i in range(3)], axis=1
    )
    bias_own = jnp.concatenate(
        [
            lax.dynamic_slice(q_bias, (head_start,), (width,)),
            jnp.zeros((width,), F32),
            lax.dynamic_slice(v_bias, (head_start,), (width,)),
        ]
    )

    def send_to_rows(blocks):
        return [blocks[0]] + [shift(blocks[r], ring, -r) for r in range(1, n_ctx)]

    def send_to_heads(blocks):
        return [blocks[0]] + [shift(blocks[r], ring, r) for r in range(1, n_ctx)]

    def order_groups(pieces, sign=1):
        back = (sign * (jnp.array(place, jnp.int32) - at)) % n_ctx
        return jnp.stack(pieces)[back]

    def heads_of(stacked):
        cols = []
        done = 0
        for group in range(n_ctx):
            lo = first_head(group)
            hi = min((group + 1) * per, n_heads)
            if hi <= done:
                continue
            cols.append(stacked[group, :, (done - lo) * HD : (hi - lo) * HD])
            done = hi
        return jnp.concatenate(cols, axis=-1)

    resid_in = tokens[0].astype(F32)
    cot_rows = cotangent[0]
    cot_full = cot_rows.astype(F32)

    def gather_group(own):
        near = flip(own, "batch")
        pair = jnp.concatenate([own, near], axis=0)
        return jnp.concatenate([pair, flip(pair, "mp")], axis=0)

    def scatter_group(partial):
        half = 2 * rows
        pair = partial[:half].astype(F32) + flip(partial[half:].astype(LOW), "mp").astype(F32)
        return pair[:rows] + flip(pair[rows:].astype(LOW), "batch").astype(F32)

    xhat_one, rstd_one = norm_parts(resid_in)
    normed_one = (xhat_one * ln1_gain + ln1_bias).astype(LOW)
    normed_all = ring_gather(normed_one, ring)
    cot_group = gather_group(cot_rows)
    w_up_own = lax.dynamic_slice(w_up, (0, batch * hid), (dim, hid))
    w_down_own = lax.dynamic_slice(w_down, (batch * hid, 0), (hid, dim))
    up_bias_own = lax.dynamic_slice(up_bias, (batch * hid,), (hid,))
    grad_hidden = dot(cot_group, w_down_own, ((1,), (1,)))

    qkv = (dot(normed_all, w_own, ((1,), (0,))) + bias_own).astype(LOW)
    attn_heads, lse = attn_forward(qkv, key_pos, query_pos)
    pieces = send_to_rows([attn_heads[r * rows : (r + 1) * rows] for r in range(n_ctx)])
    attn_rows = heads_of(order_groups(pieces))
    resid_mid = resid_in + dot(attn_rows, w_out, ((1,), (0,))) + out_bias

    xhat_two, rstd_two = norm_parts(resid_mid)
    normed_two = (xhat_two * ln2_gain + ln2_bias).astype(LOW)
    normed_group = gather_group(normed_two)
    pre_act = dot(normed_group, w_up_own, ((1,), (0,))) + up_bias_own
    tanh = jnp.tanh(GELU_C * (pre_act + GELU_A * pre_act * pre_act * pre_act))
    hidden = (0.5 * pre_act * (1.0 + tanh)).astype(LOW)
    slope = 0.5 * (1.0 + tanh) + 0.5 * pre_act * (1.0 - tanh * tanh) * GELU_C * (
        1.0 + 3.0 * GELU_A * pre_act * pre_act
    )
    grad_pre = grad_hidden * slope
    grad_pre_low = grad_pre.astype(LOW)
    grad_normed_two = scatter_group(dot(grad_pre_low, w_up_own, ((1,), (1,))))
    up_shift_grad = jnp.sum(grad_pre, axis=0)
    down_own = scatter_group(dot(hidden, w_down_own, ((1,), (0,))))
    layer_rows = (resid_mid + down_own + down_bias).astype(LOW)

    bits = []
    bit = 1
    while bit < n_ctx:
        bits.append(bit)
        bit *= 2
    dims = [2] * len(bits)

    def reduce_ctx(turned, right):
        lead = turned.shape[:-2]
        k = right.shape[1]
        left = turned.reshape((lead[0], *dims, part, turned.shape[-1]))
        axis = len(dims)
        mine = ctx & 1
        away = lax.dynamic_index_in_dim(left, 1 - mine, axis, keepdims=False)
        keep = lax.dynamic_index_in_dim(left, mine, axis, keepdims=False)
        got = flip(dot(away, right, ((away.ndim - 1,), (0,))).astype(LOW), "ctx", 1)
        value = dot(keep, right, ((keep.ndim - 1,), (0,))) + got.astype(F32)
        for level, this in enumerate(bits[1:], 1):
            axis = len(dims) - level
            mine = (ctx // this) & 1
            away = lax.dynamic_index_in_dim(value, 1 - mine, axis, keepdims=False)
            keep = lax.dynamic_index_in_dim(value, mine, axis, keepdims=False)
            value = keep + flip(away.astype(LOW), "ctx", this).astype(F32)
        return value

    def turn(left):
        return left.T.reshape(n_batch, n_ctx, part, left.shape[0])

    def join_hidden(value):
        away = lax.dynamic_index_in_dim(value, 1 - batch, 0, keepdims=False)
        keep = lax.dynamic_index_in_dim(value, batch, 0, keepdims=False)
        got = flip(away.astype(LOW), "batch").astype(F32)
        first = jnp.where(batch == 0, keep, got)
        second = jnp.where(batch == 0, got, keep)
        return jnp.concatenate([first, second], axis=-1)

    down_part = join_hidden(reduce_ctx(turn(cot_group), hidden)).T
    up_part = join_hidden(reduce_ctx(turn(normed_group), grad_pre_low))

    mid_part, gain_two_grad, shift_two_grad = norm_back(grad_normed_two, xhat_two, rstd_two, ln2_gain)
    grad_mid = cot_full + mid_part
    grad_mid_low = grad_mid.astype(LOW)
    grad_attn = dot(grad_mid_low, w_out, ((1,), (1,))).astype(LOW)
    by_group = jnp.stack(
        [grad_attn[:, first_head(g) * HD : first_head(g) * HD + width] for g in range(n_ctx)]
    )[groups]
    grad_heads = jnp.concatenate(send_to_heads([by_group[r] for r in range(n_ctx)]), axis=0)

    half = dim // n_mp
    attn_pair = jnp.concatenate([attn_rows, flip(attn_rows, "mp")], axis=0)
    mid_away = lax.dynamic_slice(grad_mid_low, (0, (1 - mp) * half), (rows, half))
    mid_keep = lax.dynamic_slice(grad_mid_low, (0, mp * half), (rows, half))
    mid_pair = jnp.concatenate([mid_keep, flip(mid_away, "mp")], axis=0)

    def reduce_batch_ctx(turned, right):
        away = lax.dynamic_index_in_dim(turned, 1 - batch, 0, keepdims=True)
        keep = lax.dynamic_index_in_dim(turned, batch, 0, keepdims=True)
        got = flip(dot(away, right, ((3,), (0,))).astype(LOW), "batch")
        value = dot(keep, right, ((3,), (0,))) + got.astype(F32)
        value = value.reshape((*dims, part, right.shape[1]))
        for level, this in enumerate(bits):
            axis = len(dims) - 1 - level
            mine = (ctx // this) & 1
            away = lax.dynamic_index_in_dim(value, 1 - mine, axis, keepdims=False)
            keep = lax.dynamic_index_in_dim(value, mine, axis, keepdims=False)
            value = keep + flip(away.astype(LOW), "ctx", this).astype(F32)
        return value

    out_part = reduce_batch_ctx(turn(attn_pair), mid_pair)

    dq, dk, dv = attn_backward(qkv, grad_heads, attn_heads, lse, key_pos, query_pos)
    pieces_q = send_to_rows([dq[r * rows : (r + 1) * rows] for r in range(n_ctx)])
    pieces_k = send_to_rows([dk[r * rows : (r + 1) * rows] for r in range(n_ctx)])
    pieces_v = send_to_rows([dv[r * rows : (r + 1) * rows] for r in range(n_ctx)])
    grad_qkv = jnp.concatenate(
        [heads_of(order_groups(pieces_q)), heads_of(order_groups(pieces_k)), heads_of(order_groups(pieces_v))],
        axis=1,
    )
    grad_normed_one = dot(grad_qkv, w_qkv, ((1,), (1,)))
    in_part, gain_one_grad, shift_one_grad = norm_back(grad_normed_one, xhat_one, rstd_one, ln1_gain)
    tokens_grad_rows = (grad_mid + in_part).astype(LOW)

    turned_one = turn(normed_all)
    outer = jnp.where(mp == 0, dq, dv)
    outer_away = jnp.where(mp == 0, dv, dq)
    right_keep = jnp.concatenate([outer, dk], axis=1)
    right_away = jnp.concatenate([outer_away, dk], axis=1)
    contract = ((3,), (0,))
    got = flip(dot(turned_one, right_away, contract).astype(LOW), "mp")
    value = dot(turned_one, right_keep, contract) + got.astype(F32)
    away = lax.dynamic_index_in_dim(value, 1 - batch, 0, keepdims=False)
    keep = lax.dynamic_index_in_dim(value, batch, 0, keepdims=False)
    value = (keep + flip(away.astype(LOW), "batch").astype(F32)).astype(LOW)
    by_dest = value[groups]
    qkv_pieces = order_groups(send_to_heads([by_dest[r] for r in range(n_ctx)]), -1)
    outer_full = heads_of(qkv_pieces[:, :, :width]).astype(F32)
    key_full = heads_of(qkv_pieces[:, :, width:]).astype(F32)
    key_half = dim // 2
    qkv_part = jnp.where(
        mp == 0,
        jnp.concatenate([outer_full, key_full[:, :key_half]], axis=1),
        jnp.concatenate([key_full[:, key_half:], outer_full], axis=1),
    )

    grad_qkv_full = grad_qkv.astype(F32)
    vectors = jnp.concatenate(
        [
            gain_one_grad,
            shift_one_grad,
            jnp.sum(grad_qkv_full[:, :dim], axis=0),
            jnp.sum(grad_qkv_full[:, 2 * dim :], axis=0),
            jnp.sum(grad_mid, axis=0),
            gain_two_grad,
            shift_two_grad,
            jnp.sum(cot_full, axis=0),
            lax.dynamic_update_slice(
                jnp.zeros((hid_half * n_mp,), F32), up_shift_grad, (mp * hid_half + batch * hid,)
            ),
        ]
    )
    everyone = ("batch", "ctx", "mp")
    n_all = n_batch * n_ctx * n_mp
    slices = lax.all_to_all(vectors.reshape(n_all, -1), everyone, split_axis=0, concat_axis=0, tiled=True)
    summed = jnp.sum(slices, axis=0)
    copies = jnp.broadcast_to(summed[None], (n_all, summed.shape[0]))
    full = lax.all_to_all(copies, everyone, split_axis=0, concat_axis=0, tiled=True).reshape(-1)
    vector_sum = full[: 8 * dim].reshape(8, dim)
    up_bias_grad = lax.dynamic_slice(full, (8 * dim + mp * hid_half,), (hid_half,))
    return (
        layer_rows[None],
        tokens_grad_rows[None],
        qkv_part,
        out_part,
        up_part,
        down_part,
        up_bias_grad,
        vector_sum,
    )


def solution(mesh):
    return jax.shard_map(
        shards,
        mesh=mesh,
        in_specs=(
            P(("batch", "mp"), "ctx", None),
            P(("batch", "mp"), "ctx", None),
            P(),
            P(),
            P(),
            P(),
            P(),
            P(),
            P(),
            P(),
            P(),
            P(),
            P(None, "mp"),
            P("mp"),
            P("mp", None),
            P(),
        ),
        out_specs=(
            P(("batch", "mp"), "ctx", None),
            P(("batch", "mp"), "ctx", None),
            P(("batch", "ctx"), "mp"),
            P(("batch", "ctx"), "mp"),
            P(("batch", "ctx"), "mp"),
            P("mp", ("batch", "ctx")),
            P("mp"),
            P(),
        ),
        check_vma=False,
    )
```

```python
import functools


import jax
import jax.numpy as jnp
from jax import lax
from jax.experimental import pallas as pl
from jax.experimental.pallas import tpu as pltpu
from jax.sharding import PartitionSpec as P

HD = 64
NORM_EPSILON = 1e-05
MASKED_SCORE = -1e30
GELU_C = 0.7978845608028654
GELU_A = 0.044715
LOW = jnp.bfloat16
BATCH, CTX, MP = "batch", "ctx", "mp"
F32 = jnp.float32
NEAR = 2


def norm_parts(rows):
    mean = jnp.mean(rows, axis=-1, keepdims=True)
    centered = rows - mean
    var = jnp.mean(centered * centered, axis=-1, keepdims=True)
    rstd = lax.rsqrt(var + NORM_EPSILON)
    return centered * rstd, rstd


def norm_back(grad, xhat, rstd, gain):
    scaled = grad * gain
    mean_one = jnp.mean(scaled, axis=-1, keepdims=True)
    mean_two = jnp.mean(scaled * xhat, axis=-1, keepdims=True)
    rows = rstd * (scaled - mean_one - xhat * mean_two)
    return rows, jnp.sum(grad * xhat, axis=0), jnp.sum(grad, axis=0)


def dot(left, right, dims):
    return lax.dot_general(left, right, (dims, ((), ())), preferred_element_type=F32)


def permute(value, axis, pairs):
    shape = value.shape
    if shape[-2] % 8 == 0:
        value = value.reshape((*shape[:-2], shape[-2] // 8, 8, shape[-1]))
    return lax.ppermute(value, axis, pairs).reshape(shape)


def flip(value, axis, bit=1):
    size = lax.axis_size(axis)
    return permute(value, axis, [(i, i ^ bit) for i in range(size)])


def ring_of(size):
    evens = list(range(0, size, 2))
    odds = list(range(1, size, 2))
    return evens + odds[::-1]


def shift(value, ring, step):
    size = len(ring)
    return permute(value, CTX, [(ring[i], ring[(i + step) % size]) for i in range(size)])


def ring_gather(own, ring):
    size = len(ring)
    half = size // 2
    ahead, behind = own, own
    blocks = [None] * size
    blocks[0] = [own]
    for step in range(1, half):
        ahead = shift(ahead, ring, 1)
        behind = shift(behind, ring, -1)
        blocks[step] = [ahead]
        blocks[size - step] = [behind]
    cut = own.shape[0] // 2
    blocks[half] = [shift(ahead[:cut], ring, 1), shift(behind[cut:], ring, -1)]
    return [piece for block in blocks for piece in block]


def call(kernel, scalars, args, outs, scratch=(), grid=(1,), in_specs=None, out_specs=None, flops=0, exps=0, after=()):
    def whole(shape):
        return pl.BlockSpec(shape, lambda *_: (0,) * len(shape))

    in_specs = in_specs or [None] * len(args)
    out_specs = out_specs or [None] * len(outs)
    in_specs = [spec or whole(arg.shape) for spec, arg in zip(in_specs, args)]
    out_specs = [spec or whole(out.shape) for spec, out in zip(out_specs, outs)]
    moved = sum(a.size * a.dtype.itemsize for a in (*args, *outs))
    if after:
        inner, first = kernel, len(scalars) + len(args)
        in_specs = in_specs + [pl.BlockSpec(memory_space=pl.ANY)] * len(after)

        def kernel(*refs):
            inner(*refs[:first], *refs[first + len(after) :])

    return pl.pallas_call(
        kernel,
        grid_spec=pltpu.PrefetchScalarGridSpec(
            num_scalar_prefetch=len(scalars),
            grid=grid,
            in_specs=in_specs,
            out_specs=out_specs,
            scratch_shapes=list(scratch),
        ),
        out_shape=list(outs),
        compiler_params=pltpu.CompilerParams(vmem_limit_bytes=56 << 20),
        cost_estimate=pl.CostEstimate(flops=flops, transcendentals=exps, bytes_accessed=moved),
    )(*scalars, *args, *after)


def array(shape, dtype=LOW):
    return jax.ShapeDtypeStruct(shape, dtype)


def row(vector):
    return vector[None, :]


def norm_in(tokens, gain, shift_by):
    def kernel(x_ref, gain_ref, shift_ref, o_ref):
        xhat, _ = norm_parts(x_ref[0].astype(F32))
        o_ref[...] = (xhat * row(gain_ref[...]) + row(shift_ref[...])).astype(LOW)

    return call(kernel, (), (tokens, gain, shift_by), [array(tokens.shape[1:])])[0]


def pack(pieces, after=()):
    def kernel(*refs):
        at = 0
        for ref in refs[:-1]:
            refs[-1][at : at + ref.shape[0], :] = ref[...]
            at += ref.shape[0]

    rows = sum(piece.shape[0] for piece in pieces)
    return call(kernel, (), pieces, [array((rows, pieces[0].shape[1]))], after=after)[0]


def project_qkv(order, pieces, weight, bias, blk, after=()):
    total = sum(piece.shape[0] for piece in pieces)
    width = weight.shape[1]

    def kernel(order_ref, *refs):
        ins, (w_ref, b_ref, qkv_ref, all_ref) = refs[: len(pieces)], refs[len(pieces) :]
        at = 0
        for ref in ins:
            all_ref[at : at + ref.shape[0], :] = ref[...]
            at += ref.shape[0]
        step = min(512, total)
        for start in range(0, total, step):
            out = dot(all_ref[start : start + step, :], w_ref[...], ((1,), (0,))) + b_ref[...]
            for part in range(step // blk):
                to = pl.multiple_of(order_ref[start // blk + part] * blk, blk)
                qkv_ref[pl.ds(to, blk), :] = out[part * blk : (part + 1) * blk].astype(LOW)

    return call(
        kernel,
        (order,),
        (*pieces, weight, bias),
        [array((total, width)), array((total, weight.shape[0]))],
        flops=2 * total * width * weight.shape[0],
        after=after,
    )


def lanes_of(shape, axis, head):
    lane = lax.broadcasted_iota(jnp.int32, shape, axis)
    return (lane >= head * HD) & (lane < (head + 1) * HD)


def attn_sizes(rows, width):
    heads = 2 if (width // HD) % 2 == 0 else 1
    block = heads * HD
    tile = min(512, rows)
    return heads, block, width // block, tile, rows // tile


def for_tiles(tile, tiles, body):
    if tiles > 4:
        body(tile * tiles)
        return
    for t in range(tiles):
        pl.when(pl.program_id(1) == t)(functools.partial(body, (t + 1) * tile))


def lanes_at(base, group, block, groups):
    if groups == 1:
        return slice(base, base + block)
    return pl.ds(pl.multiple_of(base + group * block, block), block)


def masked(scores, fill, tiles):
    keys, tile = scores.shape
    first = 0 if tiles > 4 else keys - tile
    key = lax.broadcasted_iota(jnp.int32, (keys - first, tile), 0) + first
    query = lax.broadcasted_iota(jnp.int32, (keys - first, tile), 1) + pl.program_id(1) * tile
    last = jnp.where(key <= query, scores[first:], fill)
    return jnp.concatenate([scores[:first], last], axis=0) if first else last


def attn_forward(order, sources, qkv, rows, blk, after=()):
    total, width = qkv.shape[0], qkv.shape[1] // 3
    heads, block, groups, tile, tiles = attn_sizes(total, width)
    n = total // rows
    per = rows // blk

    def kernel(order_ref, sources_ref, qkv_ref, *refs):
        outs_ref, lse_ref, sorted_ref = refs[0], refs[-2], refs[-1]
        group, t = pl.program_id(0), pl.program_id(1)
        at = lanes_at(0, group, block, groups)
        first = pl.multiple_of(t * tile, tile)
        queries = qkv_ref[pl.ds(first, tile), at] * LOW(HD**-0.5)

        def body(keys_seen):
            keys = qkv_ref[:keys_seen, lanes_at(width, group, block, groups)]
            values = qkv_ref[:keys_seen, lanes_at(2 * width, group, block, groups)]
            total_out = None
            for head in range(heads):
                part = jnp.where(lanes_of(queries.shape, 1, head), queries, LOW(0))
                scores = masked(dot(keys, part, ((1,), (1,))), MASKED_SCORE, tiles)
                top = jnp.max(scores, axis=0, keepdims=True)
                weights = jnp.exp(scores - top)
                mass = jnp.sum(weights, axis=0, keepdims=True)
                lse_ref[group, t, head : head + 1, :] = top + jnp.log(mass)
                out = dot(values, weights.astype(LOW), ((0,), (0,))) * (1.0 / mass)
                total_out = out if head == 0 else jnp.where(lanes_of(out.shape, 0, head), out, total_out)
            sorted_ref[pl.ds(first, tile), at] = total_out.T.astype(LOW)

        for_tiles(tile, tiles, body)

        @pl.when((group == groups - 1) & (t == tiles - 1))
        def _():
            for r in range(n):
                for i in range(per):
                    source = pl.multiple_of(order_ref[r * per + i] * blk, blk)
                    outs_ref[sources_ref[r], i * blk : (i + 1) * blk, :] = sorted_ref[pl.ds(source, blk), :]

    results = call(
        kernel,
        (order, sources),
        (qkv,),
        [array((n, rows, width)), array((groups, tiles, heads, tile), F32)],
        scratch=[pltpu.VMEM((total, width), LOW)],
        grid=(groups, tiles),
        flops=4 * total * total * width,
        exps=total * total * width // HD,
        after=after,
    )
    return results


def attn_backward(order, sources, qkv, grads, outs, lse, rows, blk, after=()):
    total, width = qkv.shape[0], qkv.shape[1] // 3
    heads, block, groups, tile, tiles = attn_sizes(total, width)
    n = total // rows
    per = rows // blk

    def kernel(order_ref, sources_ref, qkv_ref, lse_ref, g_ref, o_ref, *refs):
        d_refs = refs[:n]
        g_all, o_all, dq_all, k_acc, v_acc, d_all = refs[n:]
        group, t = pl.program_id(0), pl.program_id(1)
        at = lanes_at(0, group, block, groups)
        first = pl.multiple_of(t * tile, tile)

        @pl.when((group == 0) & (t == 0))
        def _():
            for r in range(n):
                for i in range(per):
                    to = pl.multiple_of(order_ref[r * per + i] * blk, blk)
                    g_all[pl.ds(to, blk), :] = g_ref[sources_ref[r], i * blk : (i + 1) * blk, :]
                    o_all[pl.ds(to, blk), :] = o_ref[sources_ref[r], i * blk : (i + 1) * blk, :]

        @pl.when(t == 0)
        def _():
            k_acc[...] = jnp.zeros_like(k_acc)
            v_acc[...] = jnp.zeros_like(v_acc)

        queries = qkv_ref[pl.ds(first, tile), at] * LOW(HD**-0.5)
        grads_here = g_all[pl.ds(first, tile), at]
        product = (grads_here.astype(F32) * o_all[pl.ds(first, tile), at].astype(F32)).T

        def body(seen):
            keys = qkv_ref[:seen, lanes_at(width, group, block, groups)]
            values = qkv_ref[:seen, lanes_at(2 * width, group, block, groups)]
            total_out = None
            for head in range(heads):
                pick = lanes_of(queries.shape, 1, head)
                part = jnp.where(pick, queries, LOW(0))
                grad = jnp.where(pick, grads_here, LOW(0))
                delta = jnp.sum(product[head * HD : (head + 1) * HD, :], axis=0, keepdims=True)
                scores = dot(keys, part, ((1,), (1,)))
                probs = masked(jnp.exp(scores - lse_ref[group, t, head : head + 1, :]), 0.0, tiles)
                back = dot(values, grad, ((1,), (1,)))
                inner = (probs * (back - delta)).astype(LOW)
                v_acc[:seen, :] += dot(probs.astype(LOW), grad, ((1,), (0,)))
                k_acc[:seen, :] += dot(inner, part, ((1,), (0,)))
                out = dot(keys, inner, ((0,), (0,)))
                total_out = out if head == 0 else jnp.where(lanes_of(out.shape, 0, head), out, total_out)
            dq_all[pl.ds(first, tile), :] = (total_out * (HD**-0.5)).T

        for_tiles(tile, tiles, body)

        @pl.when(t == tiles - 1)
        def _():
            for part, ref in enumerate((dq_all, k_acc, v_acc)):
                d_all[:, lanes_at(part * width, group, block, groups)] = ref[...].astype(LOW)

        @pl.when((group == groups - 1) & (t == tiles - 1))
        def _():
            for r in range(n):
                for i in range(per):
                    source = pl.multiple_of(order_ref[r * per + i] * blk, blk)
                    d_refs[r][i * blk : (i + 1) * blk, :] = d_all[pl.ds(source, blk), :]

    return call(
        kernel,
        (order, sources),
        (qkv, lse, grads, outs),
        [array((rows, 3 * width))] * n,
        scratch=[
            pltpu.VMEM((total, width), LOW),
            pltpu.VMEM((total, width), LOW),
            pltpu.VMEM((total, block), F32),
            pltpu.VMEM((total, block), F32),
            pltpu.VMEM((total, block), F32),
            pltpu.VMEM((total, 3 * width), LOW),
        ],
        grid=(groups, tiles),
        flops=10 * total * total * width,
        exps=total * total * width // HD,
        after=after,
    )


def owned(spans, group, n_heads):
    low = spans[group]
    high = spans[group + 1] if group + 1 < len(spans) else n_heads
    return (high - low) * HD, low * HD


def project_out(spans, pieces, weight, tokens, vectors, after=()):
    rows, dim = tokens.shape[1:]
    n = len(spans)
    n_heads = dim // HD

    def kernel(in_ref, w_ref, x_ref, bias_ref, gain_ref, shift_ref, attn_ref, mid_ref, normed_ref):
        for group in range(n):
            size, lane = owned(spans, group, n_heads)
            if size:
                attn_ref[:, lane : lane + size] = in_ref[group, :, :size]
        mid = x_ref[0].astype(F32) + dot(attn_ref[...], w_ref[...], ((1,), (0,)))
        mid = mid + row(bias_ref[...])
        mid_ref[...] = mid
        xhat, _ = norm_parts(mid)
        normed_ref[...] = (xhat * row(gain_ref[...]) + row(shift_ref[...])).astype(LOW)

    return call(
        kernel,
        (),
        (pieces, weight, tokens, *vectors),
        [array((rows, dim)), array((rows, dim), F32), array((rows, dim))],
        flops=2 * rows * dim * dim,
        after=after,
    )


def feed(normed, weight, bias, grad_hidden, out_dtype, after=()):
    rows, dim = normed.shape
    hid = weight.shape[1]
    step = min(128, rows)

    def kernel(x_ref, w_ref, b_ref, gh_ref, hidden_ref, grad_ref, out_ref, sum_ref):
        total = None
        for at in range(0, rows, step):
            here = slice(at, at + step)
            v = dot(x_ref[here, :], w_ref[...], ((1,), (0,))) + row(b_ref[...])
            square = v * v
            tanh = jnp.tanh(GELU_C * (v + GELU_A * (square * v)))
            half_one = 0.5 * (1.0 + tanh)
            hidden_ref[here, :] = (v * half_one).astype(LOW)
            slope = half_one + 0.5 * v * (1.0 - tanh * tanh) * GELU_C * (1.0 + 3.0 * GELU_A * square)
            grad = gh_ref[here, :] * slope
            low = grad.astype(LOW)
            grad_ref[here, :] = low
            column = jnp.sum(grad, axis=0, keepdims=True)
            total = column if total is None else total + column
        sum_ref[...] = total
        out_ref[...] = dot(grad_ref[...], w_ref[...], ((1,), (1,))).astype(out_dtype)

    return call(
        kernel,
        (),
        (normed, weight, bias, grad_hidden),
        [array((rows, hid)), array((rows, hid)), array((rows, dim), out_dtype), array((1, hid), F32)],
        flops=4 * rows * dim * hid,
        exps=rows * hid,
        after=after,
    )


def feed_dot(left, right, turned, out_dtype, after=()):
    rows, width = left.shape[0], right.shape[0 if turned else 1]

    def kernel(x_ref, w_ref, out_ref):
        dims = ((1,), (1,)) if turned else ((1,), (0,))
        out_ref[...] = dot(x_ref[...], w_ref[...], dims).astype(out_dtype)

    flops = 2 * left.size * width
    return call(kernel, (), (left, right), [array((rows, width), out_dtype)], flops=flops, after=after)[0]


def halve(mine, keep, got, splits, after=()):
    lead, tail = splits
    _, fill, k = keep.shape

    def kernel(mine_ref, keep_ref, got_ref, away_ref, out_ref):
        for i in range(lead):
            stay = (2 * i + mine_ref[0]) * tail
            go = (2 * i + 1 - mine_ref[0]) * tail
            for j in range(tail):
                away_ref[i * tail + j] = (keep_ref[go + j].astype(F32) + got_ref[go + j].astype(F32)).astype(LOW)
                out_ref[i * tail + j] = (keep_ref[stay + j].astype(F32) + got_ref[stay + j].astype(F32)).astype(LOW)

    outs = [array((lead * tail, fill, k)), array((lead * tail, fill, k))]
    return call(kernel, (mine.reshape(1),), (keep, got), outs, after=after)


def add_blocks(keep, got, out_dtype, part, after=()):
    blocks, _, k = keep.shape

    def kernel(keep_ref, got_ref, out_ref):
        for i in range(blocks):
            out_ref[i] = (keep_ref[i, :part, :].astype(F32) + got_ref[i, :part, :].astype(F32)).astype(out_dtype)

    return call(kernel, (), (keep, got), [array((blocks, part, k), out_dtype)], after=after)[0]


def padded(part):
    return -(-part // 8) * 8


def weight_grad(mine, lefts, rights, part, splits, after=()):
    fill = padded(part)
    dim, k = lefts[0].shape[1], rights[0].shape[1]
    lead, tail = splits
    count = len(lefts)

    def kernel(mine_ref, *refs):
        ls, rs = refs[:count], refs[count : 2 * count]
        away_ref, keep_ref, acc_ref = refs[2 * count :]
        step = 256
        for at in range(0, dim, step):
            end = min(at + step, dim)
            value = dot(ls[0][:, at:end], rs[0][...], ((0,), (0,)))
            for left, right in zip(ls[1:], rs[1:]):
                value += dot(left[:, at:end], right[...], ((0,), (0,)))
            acc_ref[at:end, :] = value
        for side in range(2):

            @pl.when(mine_ref[0] == side)
            def _():
                for i in range(lead):
                    for j in range(tail):
                        keep = ((2 * i + side) * tail + j) * part
                        away = ((2 * i + 1 - side) * tail + j) * part
                        keep_ref[i * tail + j, :part, :] = acc_ref[keep : keep + part, :].astype(LOW)
                        away_ref[i * tail + j, :part, :] = acc_ref[away : away + part, :].astype(LOW)
                        if part < fill:
                            keep_ref[i * tail + j, part:, :] = jnp.zeros((fill - part, k), LOW)
                            away_ref[i * tail + j, part:, :] = jnp.zeros((fill - part, k), LOW)

    rows = sum(left.shape[0] for left in lefts)
    return call(
        kernel,
        (mine.reshape(1),),
        (*lefts, *rights),
        [array((lead * tail, fill, k)), array((lead * tail, fill, k))],
        scratch=[pltpu.VMEM((dim, k), F32)],
        flops=2 * rows * dim * k,
        after=after,
    )


def join_feed(member, keep, far, got, part):
    _, _, hid = keep.shape

    def kernel(member_ref, keep_ref, far_ref, got_ref, out_ref):
        for who in range(4):

            @pl.when(member_ref[0] == who)
            def _():
                views = (
                    (who, keep_ref.at[who % 2]),
                    (who ^ 2, far_ref.at[who % 2]),
                    (who ^ 1, got_ref.at[0]),
                    (who ^ 3, got_ref.at[1]),
                )
                for place, ref in views:
                    out_ref[:, place * hid : (place + 1) * hid] = ref[:part, :].astype(F32)

    return call(kernel, (member.reshape(1),), (keep, far, got), [array((part, 4 * hid), F32)])[0]


def qkv_grad(mp, normed, pieces, part, after=()):
    total, dim = normed.shape
    n = len(pieces)
    rows, width = pieces[0].shape[0], pieces[0].shape[1] // 3
    blocks = dim // part
    fill = padded(part)

    def kernel(mp_ref, x_ref, *refs):
        ins = refs[:n]
        away_ref, keep_ref, sum_ref, all_ref, acc_ref = refs[n:]
        for r in range(n):
            all_ref[r * rows : (r + 1) * rows, :] = ins[r][...]
        sum_ref[...] = jnp.sum(all_ref[...].astype(F32), axis=0, keepdims=True)
        step = 256
        for at in range(0, dim, step):
            end = min(at + step, dim)
            acc_ref[at:end, :] = dot(x_ref[:, at:end], all_ref[...], ((0,), (0,)))
        for side in range(2):

            @pl.when(mp_ref[0] == side)
            def _():
                for i in range(blocks):
                    here = slice(i * part, (i + 1) * part)
                    away = slice((1 - side) * width, (3 - side) * width)
                    keep_ref[i, :part, :] = acc_ref[here, side * width : (side + 2) * width].astype(LOW)
                    away_ref[i, :part, :] = acc_ref[here, away].astype(LOW)
                    if part < fill:
                        keep_ref[i, part:, :] = jnp.zeros((fill - part, 2 * width), LOW)
                        away_ref[i, part:, :] = jnp.zeros((fill - part, 2 * width), LOW)

    return call(
        kernel,
        (mp.reshape(1),),
        (normed, *pieces),
        [
            array((blocks, fill, 2 * width)),
            array((blocks, fill, 2 * width)),
            array((1, 3 * width), F32),
        ],
        scratch=[pltpu.VMEM((total, 3 * width), LOW), pltpu.VMEM((dim, 3 * width), F32)],
        flops=6 * total * dim * width,
        after=after,
    )


def join_qkv(mp, spans, received, dim, part):
    n, _, double = received.shape
    width = double // 2
    n_heads = dim // HD
    cut = dim // 2

    def kernel(mp_ref, in_ref, out_ref):
        for side in range(2):

            @pl.when(mp_ref[0] == side)
            def _():
                for group in range(n):
                    size, lane = owned(spans, group, n_heads)
                    if not size:
                        continue
                    for first, start in ((0, 0 if side == 0 else -cut), (width, dim if side == 0 else cut)):
                        low = max(start + lane, 0)
                        high = min(start + lane + size, dim + cut)
                        if low < high:
                            source = first + low - start - lane
                            out_ref[:, low:high] = in_ref[group, :part, source : source + high - low].astype(F32)

    return call(kernel, (mp.reshape(1),), (received,), [array((part, dim + cut), F32)])[0]


def finish_vectors(mp, late, sizes, spans, dim, hid_half, width, slice_size):
    n_batch, n_ctx, n_mp = sizes
    n_heads = dim // HD
    across = dim // slice_size

    def kernel(mp_ref, in_ref, out_ref, up_ref):
        terms = jnp.sum(in_ref[:, : 2 * dim].astype(F32), axis=0, keepdims=True)
        out_ref[0:1, :] = terms[:, :dim]
        out_ref[1:2, :] = terms[:, dim:]
        for group in range(n_ctx):
            size, lane = owned(spans, group, n_heads)
            if not size:
                continue
            total = jnp.zeros((1, 2 * width), F32)
            for batch in range(n_batch):
                for core in range(n_mp):
                    who = (batch * n_ctx + group) * n_mp + core
                    total += in_ref[who : who + 1, 2 * dim : 2 * dim + 2 * width].astype(F32)
            out_ref[2:3, lane : lane + size] = total[:, :size]
            out_ref[3:4, lane : lane + size] = total[:, width : width + size]
        first = 2 * dim + 2 * width
        high = in_ref[:, first : first + slice_size].astype(F32)
        early = high + in_ref[:, first + slice_size : first + 2 * slice_size].astype(F32)
        for i in range(4 * across):
            to = (i % across) * slice_size
            out_ref[4 + i // across : 5 + i // across, to : to + slice_size] = early[i : i + 1, :]
        for side in range(n_mp):

            @pl.when(mp_ref[0] == side)
            def _():
                for i in range(hid_half // slice_size):
                    at = 4 * across + side * (hid_half // slice_size) + i
                    up_ref[:, i * slice_size : (i + 1) * slice_size] = early[at : at + 1, :]

    results = call(kernel, (mp.reshape(1),), (late,), [array((8, dim), F32), array((1, hid_half), F32)])
    return results[0], results[1].reshape(-1)


def scatter_first(keep, got, rows, after=()):
    dim = keep.shape[1]
    half = rows // 2

    def kernel(keep_ref, got_ref, one_ref, two_ref, own_ref, side_ref):
        def some(first, count):
            return keep_ref[first : first + count, :] + got_ref[first : first + count, :].astype(F32)

        one_ref[...] = some(3 * rows, half).astype(LOW)
        two_ref[...] = some(3 * rows + half, half).astype(LOW)
        own_ref[...] = some(0, rows)
        side_ref[0] = some(rows, rows)
        side_ref[1] = some(2 * rows, rows)

    outs = [array((half, dim)), array((half, dim)), array((rows, dim), F32), array((2, rows, dim), F32)]
    return call(kernel, (), (keep, got), outs, after=after)


def scatter_second(side, one, two, after=()):
    _, rows, dim = side.shape
    half = rows // 2

    def kernel(side_ref, one_ref, two_ref, batch_ref, near_ref):
        batch_ref[:half, :] = (side_ref[0, :half, :] + one_ref[...].astype(F32)).astype(LOW)
        batch_ref[half:, :] = side_ref[0, half:, :].astype(LOW)
        near_ref[:half, :] = side_ref[1, :half, :].astype(LOW)
        near_ref[half:, :] = (side_ref[1, half:, :] + two_ref[...].astype(F32)).astype(LOW)

    return call(kernel, (), (side, one, two), [array((rows, dim)), array((rows, dim))], after=after)


def finish_out(mid, acc, one, two, bias, after=()):
    rows, dim = mid.shape

    def kernel(mid_ref, acc_ref, one_ref, two_ref, bias_ref, out_ref):
        own = acc_ref[...] + one_ref[...].astype(F32) + two_ref[...].astype(F32)
        out_ref[0] = (mid_ref[...] + own + row(bias_ref[...])).astype(LOW)

    return call(kernel, (), (mid, acc, one, two, bias), [array((1, rows, dim))], after=after)[0]


def back_out(mp, spans, width, summed, mid, cot, gain, weight):
    acc, one, two = summed
    rows, dim = mid.shape
    n = len(spans)
    cols = dim // 2

    def kernel(mp_ref, acc_ref, one_ref, two_ref, mid_ref, cot_ref, gain_ref, w_ref, *refs):
        grad_ref, keep_ref, away_ref, sums_ref, outs_ref, full_ref, turned_ref = refs
        full_ref[...] = acc_ref[...] + one_ref[...].astype(F32) + two_ref[...].astype(F32)
        xhat, rstd = norm_parts(mid_ref[...])
        back, gain_grad, shift_grad = norm_back(full_ref[...], xhat, rstd, row(gain_ref[...]))
        cot_full = cot_ref[0].astype(F32)
        grad = cot_full + back
        grad_ref[...] = grad
        low = grad.astype(LOW)
        for side in range(2):

            @pl.when(mp_ref[0] == side)
            def _():
                keep_ref[...] = low[:, side * cols : (side + 1) * cols]
                away_ref[...] = low[:, (1 - side) * cols : (2 - side) * cols]

        sums_ref[0:1, :] = jnp.sum(grad, axis=0, keepdims=True)
        sums_ref[1:2, :] = row(gain_grad)
        sums_ref[2:3, :] = row(shift_grad)
        sums_ref[3:4, :] = jnp.sum(cot_full, axis=0, keepdims=True)
        turned_ref[...] = dot(w_ref[...], low, ((1,), (1,)))
        for group in range(n):
            first = spans[group] * HD
            outs_ref[group] = turned_ref[first : first + width, :].T.astype(LOW)

    return call(
        kernel,
        (mp.reshape(1),),
        (acc, one, two, mid, cot, gain, weight),
        [
            array((rows, dim), F32),
            array((rows, cols)),
            array((rows, cols)),
            array((4, dim), F32),
            array((n, rows, width)),
        ],
        scratch=[pltpu.VMEM((rows, dim), F32), pltpu.VMEM((dim, rows), F32)],
        flops=2 * rows * dim * dim,
    )


def back_qkv(groups, spans, pieces, weight, tokens, gain, grad_mid, after=()):
    rows, dim = tokens.shape[1:]
    n = len(pieces)
    n_heads = dim // HD
    width = pieces[0].shape[1] // 3
    steps = 5 if dim % 40 == 0 else 1
    chunk = dim // steps

    def kernel(groups_ref, *refs):
        ins = refs[:n]
        w_ref, x_ref, gain_ref, mid_ref, out_ref, vec_ref, all_ref, part_ref = refs[n:]
        step = pl.program_id(0)

        @pl.when(step == 0)
        def _():
            for r in range(n):
                for group in range(n):
                    size, lane = owned(spans, group, n_heads)
                    if not size:
                        continue

                    @pl.when(groups_ref[r] == group)
                    def _():
                        for part in range(3):
                            all_ref[:, part * dim + lane : part * dim + lane + size] = ins[r][
                                :, part * width : part * width + size
                            ]

        part_ref[pl.ds(pl.multiple_of(step * chunk, 8), chunk), :] = dot(w_ref[...], all_ref[...], ((1,), (1,)))

        @pl.when(step == steps - 1)
        def _():
            xhat, rstd = norm_parts(x_ref[0].astype(F32))
            back, gain_grad, shift_grad = norm_back(part_ref[...].T, xhat, rstd, row(gain_ref[...]))
            out_ref[0] = (mid_ref[...] + back).astype(LOW)
            vec_ref[0:1, :] = row(gain_grad)
            vec_ref[1:2, :] = row(shift_grad)

    in_specs = [None] * n + [pl.BlockSpec((chunk, 3 * dim), lambda i, *_: (i, 0))] + [None] * 3
    return call(
        kernel,
        (groups,),
        (*pieces, weight, tokens, gain, grad_mid),
        [array((1, rows, dim)), array((2, dim), F32)],
        scratch=[
            pltpu.VMEM((rows, 3 * dim), LOW),
            pltpu.VMEM((dim, rows), F32),
        ],
        grid=(steps,),
        in_specs=in_specs,
        flops=6 * rows * dim * dim,
        after=after,
    )


def layer(
    tokens, cotangent, block_table, w_qkv, q_bias, v_bias, w_out, out_bias,
    ln1_gain, ln1_bias, ln2_gain, ln2_bias, w_up, up_bias, w_down, down_bias,
):
    n_ctx, n_mp, n_batch = lax.axis_size(CTX), lax.axis_size(MP), lax.axis_size(BATCH)
    ctx, mp, batch = lax.axis_index(CTX), lax.axis_index(MP), lax.axis_index(BATCH)
    rows, dim = tokens.shape[1], tokens.shape[2]
    total = rows * n_ctx
    blk = total // block_table.shape[0]
    n_heads = dim // HD
    per = -(-n_heads // n_ctx)
    width = per * HD
    hid_half = w_up.shape[1]
    near = (ctx // NEAR) % 2
    member = batch * 2 + near
    hid = hid_half // (2 * n_batch)
    part = dim // (n_batch * n_ctx)
    half = rows // 2
    spans = [group * (n_heads - per) // (n_ctx - 1) for group in range(n_ctx)]

    ring = ring_of(n_ctx)
    place = [ring.index(i) for i in range(n_ctx)]
    ring_arr = jnp.array(ring, jnp.int32)
    at = jnp.array(place, jnp.int32)[ctx]
    steps = jnp.arange(n_ctx, dtype=jnp.int32)
    sources = ring_arr[(at - steps) % n_ctx]
    groups = ring_arr[(at + steps) % n_ctx]
    blocks_per = rows // blk
    order = block_table.reshape(n_ctx, blocks_per)[sources].reshape(-1)

    starts_of = jnp.array(spans, jnp.int32) * HD
    head_start = starts_of[ctx]
    w_own = jnp.concatenate(
        [lax.dynamic_slice(w_qkv, (0, head_start + i * dim), (dim, width)) for i in range(3)], axis=1
    )
    bias_own = jnp.concatenate(
        [
            lax.dynamic_slice(q_bias, (head_start,), (width,)),
            jnp.zeros((width,), F32),
            lax.dynamic_slice(v_bias, (head_start,), (width,)),
        ]
    )

    def send_to_rows(blocks):
        return [blocks[0]] + [shift(blocks[r], ring, -r) for r in range(1, n_ctx)]

    def gather_first(own, own_near):
        return flip(own, BATCH, 1), flip(own_near, CTX, NEAR)

    def gather_second(sides):
        return flip(sides[0][:half], CTX, NEAR), flip(sides[1][half:], BATCH, 1)

    def exchange(blocks):
        return lax.all_to_all(blocks, CTX, split_axis=0, concat_axis=0, tiled=True)

    normed_pieces = ring_gather(norm_in(tokens, ln1_gain, ln1_bias), ring)
    w_down_own = lax.dynamic_slice(w_down.T, (0, member * hid), (dim, hid))
    up_bias_own = lax.dynamic_slice(up_bias, (member * hid,), (hid,))
    qkv, normed_all = project_qkv(order, normed_pieces, w_own, row(bias_own), blk, (w_down_own, up_bias_own))

    cot_own = cotangent[0]
    cot_near, _ = lax.optimization_barrier((cot_own, normed_pieces[n_ctx // 2]))
    cot_sides = gather_first(cot_own, cot_near)
    attn_heads, lse = attn_forward(order, sources, qkv, rows, blk)
    attn_pieces = exchange(attn_heads)
    cot_chip = pack([cot_own, *cot_sides, *gather_second(cot_sides)], (lse,))
    cot_groups = cot_chip, flip(cot_chip, MP, 1)
    attn_rows, resid_mid, normed_two = project_out(
        spans, attn_pieces, w_out, tokens, (out_bias, ln2_gain, ln2_bias), (cot_chip,)
    )

    near_rows = gather_first(normed_two, normed_two)
    far_rows = gather_second(near_rows)
    w_up_later, _ = lax.optimization_barrier((w_up, normed_two))
    w_up_own = lax.dynamic_slice(w_up_later, (0, member * hid), (dim, hid))
    hidden_back_keep = feed_dot(cot_groups[0], w_down_own, False, F32, (normed_two,))
    normed_chip = pack([normed_two, *near_rows, *far_rows], (hidden_back_keep,))
    normed_groups = normed_chip, flip(normed_chip, MP, 1)
    hidden_back_away = feed_dot(cot_groups[1], w_down_own, False, F32, (normed_chip,))
    hidden_away, low_away, back_away, sum_away = feed(normed_groups[1], w_up_own, up_bias_own, hidden_back_away, LOW)
    hidden_keep, low_keep, back_keep, sum_keep = feed(
        normed_groups[0], w_up_own, up_bias_own, hidden_back_keep, F32, (back_away,)
    )
    one, two, acc, side = scatter_first(back_keep, flip(back_away, MP, 1), rows)
    one_got, two_got = flip(one, CTX, NEAR), flip(two, BATCH, 1)
    by_batch, by_near = scatter_second(side, one_got, two_got)
    down_away = feed_dot(hidden_away, w_down_own, True, LOW, (by_near,))
    grad_normed_two = acc, flip(by_batch, BATCH, 1), flip(by_near, CTX, NEAR)
    up_shift_grad = (sum_keep + sum_away).reshape(-1)

    grad_mid, mid_keep, mid_away, mid_vectors, by_group = back_out(
        mp, spans, width, grad_normed_two, resid_mid, cotangent, ln2_gain, w_out
    )
    grad_heads = exchange(by_group)

    bits = []
    bit = 1
    while bit < n_ctx:
        bits.append(bit)
        bit *= 2
    fill = padded(part)

    def feed_grad(lefts, rights, after):
        away, keep = weight_grad(ctx % 2, lefts, rights, part, (n_batch * n_ctx // 2, 1), after)
        return flip(away, CTX, 1), keep

    def feed_half(got, keep, after=()):
        left = [bit for bit in reversed(bits) if bit > 1]
        halves = [bit for bit in bits if bit > 1 and bit != NEAR]
        first = None
        for bit in halves:
            lead = n_batch * 2 ** left.index(bit)
            tail = 2 ** (len(left) - 1 - left.index(bit))
            away, keep = halve((ctx // bit) % 2, keep, got, (lead, tail), after if first is None else ())
            first = away if first is None else first
            got = flip(away, CTX, bit)
            left.remove(bit)
        return first, got, keep

    def feed_swap(got, keep, after=()):
        away, keep = halve(batch, keep, got, (1, 2), after)
        far = flip(away, BATCH, 1)
        other = jnp.stack([lax.dynamic_index_in_dim(x, 1 - near, 0, keepdims=False) for x in (keep, far)])
        return away, (keep, far, flip(other, CTX, NEAR))

    down_got, down_kept = feed_grad(cot_groups, (hidden_keep, hidden_away), (one,))
    up_got, up_kept = feed_grad(normed_groups, (low_keep, low_away), (grad_mid,))

    down_first, down_got, down_kept = feed_half(down_got, down_kept, (up_kept,))

    out_away, out_kept = weight_grad(
        batch, (attn_rows, flip(attn_rows, MP)), (mid_keep, flip(mid_away, MP)), part, (1, n_ctx), (down_first,)
    )
    out_got = flip(out_away, BATCH, 1)

    everyone = (BATCH, CTX, MP)
    n_all = n_batch * n_ctx * n_mp
    early = jnp.concatenate(
        [
            mid_vectors.reshape(-1),
            lax.dynamic_update_slice(
                jnp.zeros((hid_half * n_mp,), F32), up_shift_grad, (mp * hid_half + member * hid,)
            ),
        ]
    )
    early, _ = lax.optimization_barrier((early, grad_heads))
    slices = lax.all_to_all(early.reshape(n_all, -1), everyone, split_axis=0, concat_axis=0, tiled=True)
    early_sum = jnp.sum(slices, axis=0)
    early_high = early_sum.astype(LOW)
    early_low = (early_sum - early_high.astype(F32)).astype(LOW)

    grad_pieces = attn_backward(order, sources, qkv, grad_heads, attn_heads, lse, rows, blk, (out_kept,))
    pieces_back = send_to_rows(grad_pieces)

    up_first, up_got, up_kept = feed_half(up_got, up_kept, (grad_pieces[0],))
    qkv_away, qkv_kept, column_sums = qkv_grad(mp, normed_all, grad_pieces, part, (up_first,))
    qkv_got = flip(qkv_away, MP, 1)

    def out_half(level, out_got, out_kept, after=()):
        bit = bits[level]
        splits = (2 ** (len(bits) - 1 - level), 1)
        away, keep = halve((ctx // bit) % 2, out_kept, out_got, splits, after)
        return away, flip(away, CTX, bit), keep

    out_first, out_got, out_kept = out_half(0, out_got, out_kept, (qkv_kept,))
    qkv_away, qkv_kept = halve(batch, qkv_kept, qkv_got, (1, n_ctx), (out_first,))
    qkv_got = flip(qkv_away, BATCH, 1)
    down_swap, down_parts = feed_swap(down_got, down_kept, (qkv_kept,))
    out_first, out_got, out_kept = out_half(1, out_got, out_kept, (down_swap,))

    value = add_blocks(qkv_kept, qkv_got, LOW, fill, (out_first,))
    received = exchange(value)
    tokens_grad_rows, in_vectors = back_qkv(
        groups, spans, pieces_back, w_qkv, tokens, ln1_gain, grad_mid, (value,)
    )

    late = jnp.concatenate(
        [
            in_vectors.reshape(-1).astype(LOW),
            column_sums[0, :width].astype(LOW),
            column_sums[0, 2 * width :].astype(LOW),
            early_high,
            early_low,
        ]
    )
    late = jnp.broadcast_to(late[None], (n_all, late.shape[0]))
    late, _ = lax.optimization_barrier((late, received))
    late = lax.all_to_all(late, everyone, split_axis=0, concat_axis=0, tiled=True)
    vector_sum, up_bias_grad = finish_vectors(
        mp, late, (n_batch, n_ctx, n_mp), spans, dim, hid_half, width, early_sum.shape[0]
    )

    down_keep = feed_dot(hidden_keep, w_down_own, True, F32, (in_vectors,))
    last, other, last_acc, last_side = scatter_first(down_keep, flip(down_away, MP), rows)
    _, up_parts = feed_swap(up_got, up_kept, (last_acc,))
    for level in range(2, len(bits)):
        out_first, out_got, out_kept = out_half(level, out_got, out_kept, (in_vectors,))
    last_batch, last_near = scatter_second(last_side, flip(last, CTX, NEAR), flip(other, BATCH, 1))
    layer_rows = finish_out(resid_mid, last_acc, flip(last_batch, BATCH, 1), flip(last_near, CTX, NEAR), down_bias)
    out_value = add_blocks(out_kept, out_got, F32, part)[0]
    qkv_part = join_qkv(mp, spans, received, dim, part)
    down_part = join_feed(member, *down_parts, part).T
    up_part = join_feed(member, *up_parts, part)
    return (
        layer_rows,
        tokens_grad_rows,
        qkv_part,
        out_value,
        up_part,
        down_part,
        up_bias_grad,
        vector_sum,
    )


def solution(mesh):
    return jax.shard_map(
        layer,
        mesh=mesh,
        in_specs=(
            P((BATCH, MP), CTX, None),
            P((BATCH, MP), CTX, None),
            P(),
            P(),
            P(),
            P(),
            P(),
            P(),
            P(),
            P(),
            P(),
            P(),
            P(None, MP),
            P(MP),
            P(MP, None),
            P(),
        ),
        out_specs=(
            P((BATCH, MP), CTX, None),
            P((BATCH, MP), CTX, None),
            P((BATCH, CTX), MP),
            P((BATCH, CTX), MP),
            P((BATCH, CTX), MP),
            P(MP, (BATCH, CTX)),
            P(MP),
            P(),
        ),
        check_vma=False,
    )
```

```python
import functools


import jax
import jax.numpy as jnp
from jax import lax
from jax.experimental import pallas as pl
from jax.experimental.pallas import tpu as pltpu
from jax.sharding import PartitionSpec as P

HD = 64
NORM_EPSILON = 1e-05
MASKED_SCORE = -1e30
GELU_C = 0.7978845608028654
GELU_A = 0.044715
LOW = jnp.bfloat16
BATCH, CTX, MP = "batch", "ctx", "mp"
F32 = jnp.float32
NEAR = 2


def norm_parts(rows):
    mean = jnp.mean(rows, axis=-1, keepdims=True)
    centered = rows - mean
    var = jnp.mean(centered * centered, axis=-1, keepdims=True)
    rstd = lax.rsqrt(var + NORM_EPSILON)
    return centered * rstd, rstd


def norm_back(grad, xhat, rstd, gain):
    scaled = grad * gain
    mean_one = jnp.mean(scaled, axis=-1, keepdims=True)
    mean_two = jnp.mean(scaled * xhat, axis=-1, keepdims=True)
    rows = rstd * (scaled - mean_one - xhat * mean_two)
    return rows, jnp.sum(grad * xhat, axis=0), jnp.sum(grad, axis=0)


def dot(left, right, dims):
    return lax.dot_general(left, right, (dims, ((), ())), preferred_element_type=F32)


SENT = {}


def sent(value):
    SENT[id(value)] = value
    return value


def permute(value, axis, pairs, far=False):
    shape = value.shape
    if shape[-2] % 8 == 0:
        value = value.reshape((*shape[:-2], shape[-2] // 8, 8, shape[-1]))
    value = lax.ppermute(value, axis, pairs).reshape(shape)
    return value if far else sent(value)


def flip(value, axis, bit=1, far=False):
    size = lax.axis_size(axis)
    return permute(value, axis, [(i, i ^ bit) for i in range(size)], far)


def ring_of(size):
    evens = list(range(0, size, 2))
    odds = list(range(1, size, 2))
    return evens + odds[::-1]


def shift(value, ring, step):
    size = len(ring)
    return permute(value, CTX, [(ring[i], ring[(i + step) % size]) for i in range(size)], True)


def ring_gather(own, ring):
    size = len(ring)
    half = size // 2
    ahead, behind = own, own
    blocks = [None] * size
    blocks[0] = [own]
    for step in range(1, half):
        ahead = shift(ahead, ring, 1)
        behind = shift(behind, ring, -1)
        blocks[step] = [ahead]
        blocks[size - step] = [behind]
    cut = own.shape[0] // 2
    blocks[half] = [shift(ahead[:cut], ring, 1), shift(behind[cut:], ring, -1)]
    return [piece for block in blocks for piece in block]


GRANT = [0]


def call(
    kernel, scalars, args, outs, scratch=(), grid=(1,), in_specs=None, out_specs=None, flops=0, exps=0, after=(), near=()
):
    def whole(shape):
        return pl.BlockSpec(shape, lambda *_: (0,) * len(shape))

    in_specs = in_specs or [None] * len(args)
    out_specs = out_specs or [None] * len(outs)
    in_specs = [spec or whole(arg.shape) for spec, arg in zip(in_specs, args)]
    out_specs = [spec or whole(out.shape) for spec, out in zip(out_specs, outs)]
    moved = sum(a.size * a.dtype.itemsize for a in (*args, *outs))
    args = tuple(
        arg
        if i in near or arg.size < 4096 or id(arg) in SENT
        else pltpu.with_memory_space_constraint(arg, pltpu.HBM)
        for i, arg in enumerate(args)
    )
    outs = [
        out if len(args) + i in near or out.size < 4096 else pltpu.HBM(out.shape, out.dtype)
        for i, out in enumerate(outs)
    ]
    if after:
        inner, first = kernel, len(scalars) + len(args)
        in_specs = in_specs + [pl.BlockSpec(memory_space=pl.ANY)] * len(after)

        def kernel(*refs):
            inner(*refs[:first], *refs[first + len(after) :])

    return pl.pallas_call(
        kernel,
        grid_spec=pltpu.PrefetchScalarGridSpec(
            num_scalar_prefetch=len(scalars),
            grid=grid,
            in_specs=in_specs,
            out_specs=out_specs,
            scratch_shapes=list(scratch),
        ),
        out_shape=list(outs),
        compiler_params=pltpu.CompilerParams(vmem_limit_bytes=GRANT[0]),
        cost_estimate=pl.CostEstimate(flops=flops, transcendentals=exps, bytes_accessed=moved),
    )(*scalars, *args, *after)


def tall(tile, width):
    return pl.BlockSpec((tile, width), lambda i, *_: (i, 0))


def tile_of(rows, most=256):
    return most if rows % most == 0 else rows


def array(shape, dtype=LOW):
    return jax.ShapeDtypeStruct(shape, dtype)


def row(vector):
    return vector[None, :]


def norm_in(turned, gain, shift_by):
    _, dim, rows = turned.shape

    def kernel(x_ref, gain_ref, shift_ref, rows_ref, o_ref):
        value = x_ref[0].astype(F32).T
        rows_ref[0] = value.astype(LOW)
        xhat, _ = norm_parts(value)
        o_ref[...] = (xhat * row(gain_ref[...]) + row(shift_ref[...])).astype(LOW)

    return call(kernel, (), (turned, gain, shift_by), [array((1, rows, dim)), array((rows, dim))])


def pack(pieces, after=()):
    def kernel(*refs):
        at = 0
        for ref in refs[:-1]:
            refs[-1][at : at + ref.shape[0], :] = ref[...]
            at += ref.shape[0]

    rows = sum(piece.shape[0] for piece in pieces)
    return call(kernel, (), pieces, [array((rows, pieces[0].shape[1]))], after=after)[0]


def project_qkv(order, pieces, weight, bias, blk, after=()):
    total = sum(piece.shape[0] for piece in pieces)
    width = weight.shape[1]

    def kernel(order_ref, *refs):
        ins, (w_ref, b_ref, qkv_ref, all_ref) = refs[: len(pieces)], refs[len(pieces) :]
        at = 0
        for ref in ins:
            all_ref[at : at + ref.shape[0], :] = ref[...]
            at += ref.shape[0]
        step = min(512, total)
        for start in range(0, total, step):
            out = dot(all_ref[start : start + step, :], w_ref[...], ((1,), (0,))) + b_ref[...]
            for part in range(step // blk):
                to = pl.multiple_of(order_ref[start // blk + part] * blk, blk)
                qkv_ref[pl.ds(to, blk), :] = out[part * blk : (part + 1) * blk].astype(LOW)

    return call(
        kernel,
        (order,),
        (*pieces, weight, bias),
        [array((total, width)), array((total, weight.shape[0]))],
        flops=2 * total * width * weight.shape[0],
        after=after,
    )


def lanes_of(shape, axis, head):
    lane = lax.broadcasted_iota(jnp.int32, shape, axis)
    return (lane >= head * HD) & (lane < (head + 1) * HD)


def attn_sizes(rows, width):
    heads = 2 if (width // HD) % 2 == 0 else 1
    block = heads * HD
    tile = min(512, rows)
    return heads, block, width // block, tile, rows // tile


def for_tiles(tile, tiles, body):
    if tiles > 4:
        body(tile * tiles)
        return
    for t in range(tiles):
        pl.when(pl.program_id(1) == t)(functools.partial(body, (t + 1) * tile))


def lanes_at(base, group, block, groups):
    if groups == 1:
        return slice(base, base + block)
    return pl.ds(pl.multiple_of(base + group * block, block), block)


def masked(scores, fill, tiles):
    keys, tile = scores.shape
    first = 0 if tiles > 4 else keys - tile
    key = lax.broadcasted_iota(jnp.int32, (keys - first, tile), 0) + first
    query = lax.broadcasted_iota(jnp.int32, (keys - first, tile), 1) + pl.program_id(1) * tile
    last = jnp.where(key <= query, scores[first:], fill)
    return jnp.concatenate([scores[:first], last], axis=0) if first else last


def attn_forward(order, sources, qkv, rows, blk, after=()):
    total, width = qkv.shape[0], qkv.shape[1] // 3
    heads, block, groups, tile, tiles = attn_sizes(total, width)
    n = total // rows
    per = rows // blk

    def kernel(order_ref, sources_ref, qkv_ref, *refs):
        outs_ref, lse_ref, sorted_ref = refs[0], refs[-2], refs[-1]
        group, t = pl.program_id(0), pl.program_id(1)
        at = lanes_at(0, group, block, groups)
        first = pl.multiple_of(t * tile, tile)
        queries = qkv_ref[pl.ds(first, tile), at] * LOW(HD**-0.5)

        def body(keys_seen):
            keys = qkv_ref[:keys_seen, lanes_at(width, group, block, groups)]
            values = qkv_ref[:keys_seen, lanes_at(2 * width, group, block, groups)]
            total_out = None
            for head in range(heads):
                part = jnp.where(lanes_of(queries.shape, 1, head), queries, LOW(0))
                scores = masked(dot(keys, part, ((1,), (1,))), MASKED_SCORE, tiles)
                top = jnp.max(scores, axis=0, keepdims=True)
                weights = jnp.exp(scores - top)
                mass = jnp.sum(weights, axis=0, keepdims=True)
                lse_ref[group, t, head : head + 1, :] = top + jnp.log(mass)
                out = dot(values, weights.astype(LOW), ((0,), (0,))) * (1.0 / mass)
                total_out = out if head == 0 else jnp.where(lanes_of(out.shape, 0, head), out, total_out)
            sorted_ref[pl.ds(first, tile), at] = total_out.T.astype(LOW)

        for_tiles(tile, tiles, body)

        @pl.when((group == groups - 1) & (t == tiles - 1))
        def _():
            for r in range(n):
                for i in range(per):
                    source = pl.multiple_of(order_ref[r * per + i] * blk, blk)
                    outs_ref[sources_ref[r], i * blk : (i + 1) * blk, :] = sorted_ref[pl.ds(source, blk), :]

    results = call(
        kernel,
        (order, sources),
        (qkv,),
        [array((n, rows, width)), array((groups, tiles, heads, tile), F32)],
        scratch=[pltpu.VMEM((total, width), LOW)],
        grid=(groups, tiles),
        flops=4 * total * total * width,
        exps=total * total * width // HD,
        after=after,
    )
    return results


def attn_backward(order, sources, qkv, grads, outs, lse, rows, blk, after=()):
    total, width = qkv.shape[0], qkv.shape[1] // 3
    heads, block, groups, tile, tiles = attn_sizes(total, width)
    n = total // rows
    per = rows // blk

    def kernel(order_ref, sources_ref, qkv_ref, lse_ref, g_ref, o_ref, *refs):
        d_ref, g_all, o_all, dq_all, k_acc, v_acc, d_all = refs
        group, t = pl.program_id(0), pl.program_id(1)
        at = lanes_at(0, group, block, groups)
        first = pl.multiple_of(t * tile, tile)

        @pl.when((group == 0) & (t == 0))
        def _():
            for r in range(n):
                for i in range(per):
                    to = pl.multiple_of(order_ref[r * per + i] * blk, blk)
                    g_all[pl.ds(to, blk), :] = g_ref[sources_ref[r], i * blk : (i + 1) * blk, :]
                    o_all[pl.ds(to, blk), :] = o_ref[sources_ref[r], i * blk : (i + 1) * blk, :]

        @pl.when(t == 0)
        def _():
            k_acc[...] = jnp.zeros_like(k_acc)
            v_acc[...] = jnp.zeros_like(v_acc)

        queries = qkv_ref[pl.ds(first, tile), at] * LOW(HD**-0.5)
        grads_here = g_all[pl.ds(first, tile), at]
        product = (grads_here.astype(F32) * o_all[pl.ds(first, tile), at].astype(F32)).T

        def body(seen):
            keys = qkv_ref[:seen, lanes_at(width, group, block, groups)]
            values = qkv_ref[:seen, lanes_at(2 * width, group, block, groups)]
            total_out = None
            for head in range(heads):
                pick = lanes_of(queries.shape, 1, head)
                part = jnp.where(pick, queries, LOW(0))
                grad = jnp.where(pick, grads_here, LOW(0))
                delta = jnp.sum(product[head * HD : (head + 1) * HD, :], axis=0, keepdims=True)
                scores = dot(keys, part, ((1,), (1,)))
                probs = masked(jnp.exp(scores - lse_ref[group, t, head : head + 1, :]), 0.0, tiles)
                back = dot(values, grad, ((1,), (1,)))
                inner = (probs * (back - delta)).astype(LOW)
                v_acc[:seen, :] += dot(probs.astype(LOW), grad, ((1,), (0,)))
                k_acc[:seen, :] += dot(inner, part, ((1,), (0,)))
                out = dot(keys, inner, ((0,), (0,)))
                total_out = out if head == 0 else jnp.where(lanes_of(out.shape, 0, head), out, total_out)
            dq_all[pl.ds(first, tile), :] = (total_out * (HD**-0.5)).T

        for_tiles(tile, tiles, body)

        @pl.when(t == tiles - 1)
        def _():
            for part, ref in enumerate((dq_all, k_acc, v_acc)):
                d_all[:, lanes_at(part * width, group, block, groups)] = ref[...].astype(LOW)

        @pl.when((group == groups - 1) & (t == tiles - 1))
        def _():
            for r in range(n):
                for i in range(per):
                    source = pl.multiple_of(order_ref[r * per + i] * blk, blk)
                    d_ref[sources_ref[r], i * blk : (i + 1) * blk, :] = d_all[pl.ds(source, blk), :]

    return call(
        kernel,
        (order, sources),
        (qkv, lse, grads, outs),
        [array((n, rows, 3 * width))],
        scratch=[
            pltpu.VMEM((total, width), LOW),
            pltpu.VMEM((total, width), LOW),
            pltpu.VMEM((total, block), F32),
            pltpu.VMEM((total, block), F32),
            pltpu.VMEM((total, block), F32),
            pltpu.VMEM((total, 3 * width), LOW),
        ],
        grid=(groups, tiles),
        flops=10 * total * total * width,
        exps=total * total * width // HD,
        after=after,
    )[0]


def owned(spans, group, n_heads):
    low = spans[group]
    high = spans[group + 1] if group + 1 < len(spans) else n_heads
    return (high - low) * HD, low * HD


def project_out(spans, pieces, weight, tokens, vectors, after=()):
    rows, dim = tokens.shape[1:]
    n = len(spans)
    n_heads = dim // HD

    def kernel(in_ref, w_ref, x_ref, bias_ref, gain_ref, shift_ref, attn_ref, mid_ref, normed_ref):
        for group in range(n):
            size, lane = owned(spans, group, n_heads)
            if size:
                attn_ref[:, lane : lane + size] = in_ref[group, :, :size]
        mid = x_ref[0].astype(F32) + dot(attn_ref[...], w_ref[...], ((1,), (0,)))
        mid = mid + row(bias_ref[...])
        mid_ref[...] = mid
        xhat, _ = norm_parts(mid)
        normed_ref[...] = (xhat * row(gain_ref[...]) + row(shift_ref[...])).astype(LOW)

    return call(
        kernel,
        (),
        (pieces, weight, tokens, *vectors),
        [array((rows, dim)), array((rows, dim), F32), array((rows, dim))],
        flops=2 * rows * dim * dim,
        after=after,
    )


def feed(normed, weight, bias, grad_hidden, out_dtype, after=(), near=()):
    rows, dim = normed.shape
    hid = weight.shape[1]
    tile = tile_of(rows)

    def kernel(x_ref, w_ref, b_ref, gh_ref, hidden_ref, grad_ref, out_ref, sum_ref):
        @pl.when(pl.program_id(0) == 0)
        def _():
            sum_ref[...] = jnp.zeros_like(sum_ref)

        v = dot(x_ref[...], w_ref[...], ((1,), (0,))) + row(b_ref[...])
        square = v * v
        tanh = jnp.tanh(GELU_C * (v + GELU_A * (square * v)))
        half_one = 0.5 * (1.0 + tanh)
        hidden_ref[...] = (v * half_one).astype(LOW)
        slope = half_one + 0.5 * v * (1.0 - tanh * tanh) * GELU_C * (1.0 + 3.0 * GELU_A * square)
        grad = gh_ref[...] * slope
        grad_ref[...] = grad.astype(LOW)
        sum_ref[...] += jnp.sum(grad, axis=0, keepdims=True)
        out_ref[...] = dot(grad_ref[...], w_ref[...], ((1,), (1,))).astype(out_dtype)

    return call(
        kernel,
        (),
        (normed, weight, bias, grad_hidden),
        [array((rows, hid)), array((rows, hid)), array((rows, dim), out_dtype), array((1, hid), F32)],
        grid=(rows // tile,),
        in_specs=[tall(tile, dim), None, None, tall(tile, hid)],
        out_specs=[tall(tile, hid), tall(tile, hid), tall(tile, dim), None],
        flops=4 * rows * dim * hid,
        exps=rows * hid,
        after=after,
        near=near,
    )


def feed_dot(left, right, turned, out_dtype, after=(), near=(1,)):
    rows, width = left.shape[0], right.shape[0 if turned else 1]

    def kernel(x_ref, w_ref, out_ref):
        dims = ((1,), (1,)) if turned else ((1,), (0,))
        out_ref[...] = dot(x_ref[...], w_ref[...], dims).astype(out_dtype)

    tile = tile_of(rows)
    return call(
        kernel,
        (),
        (left, right),
        [array((rows, width), out_dtype)],
        grid=(rows // tile,),
        in_specs=[tall(tile, left.shape[1]), None],
        out_specs=[tall(tile, width)],
        flops=2 * left.size * width,
        after=after,
        near=near,
    )[0]


def halve(mine, keep, got, splits, after=(), part=0, extra=0):
    lead, tail = splits
    _, fill, k = keep.shape

    def kernel(mine_ref, keep_ref, got_ref, away_ref, out_ref, *extra_refs):
        for i in range(lead):
            stay = (2 * i + mine_ref[0]) * tail
            go = (2 * i + 1 - mine_ref[0]) * tail
            for j in range(tail):
                away_ref[i * tail + j] = (keep_ref[go + j].astype(F32) + got_ref[go + j].astype(F32)).astype(LOW)
                out_ref[i * tail + j] = (keep_ref[stay + j].astype(F32) + got_ref[stay + j].astype(F32)).astype(LOW)
        for ref in extra_refs:
            for i in range(2 * lead * tail):
                row_of = keep_ref[i, part : part + 1, :].astype(F32) + got_ref[i, part : part + 1, :].astype(F32)
                ref[i : i + 1, :] = row_of[:, :extra]

    outs = [array((lead * tail, fill, k)), array((lead * tail, fill, k))]
    if extra:
        outs.append(array((2 * lead * tail, extra), F32))
    return call(kernel, (mine.reshape(1),), (keep, got), outs, after=after)


def add_blocks(ctx, keep, got, after=()):
    blocks, fill, k = keep.shape

    def kernel(ctx_ref, keep_ref, got_ref, *outs):
        for i in range(blocks):
            at = ctx_ref[0] ^ i
            outs[i][...] = (keep_ref[at].astype(F32) + got_ref[at].astype(F32)).astype(LOW)

    return call(kernel, (ctx.reshape(1),), (keep, got), [array((fill, k))] * blocks, after=after)


def join_out(keep, got, part, after=()):
    _, _, k = keep.shape

    def kernel(keep_ref, got_ref, out_ref):
        out_ref[...] = keep_ref[0, :part, :].astype(F32) + got_ref[0, :part, :].astype(F32)

    return call(kernel, (), (keep, got), [array((part, k), F32)], after=after)[0]


def padded(part):
    return (part // 8 + 1) * 8


def weight_grad(mine, lefts, rights, part, splits, after=(), extra=None):
    fill = padded(part)
    dim, k = lefts[0].shape[1], rights[0].shape[1]
    lead, tail = splits
    count = len(lefts)
    extras = () if extra is None else (extra,)

    def kernel(mine_ref, *refs):
        ls, rs = refs[:count], refs[count : 2 * count]
        away_ref, keep_ref, acc_ref = refs[-3:]
        step = 256
        for at in range(0, dim, step):
            end = min(at + step, dim)
            value = dot(ls[0][:, at:end], rs[0][...], ((0,), (0,)))
            for left, right in zip(ls[1:], rs[1:]):
                value += dot(left[:, at:end], right[...], ((0,), (0,)))
            acc_ref[at:end, :] = value
        for side in range(2):

            @pl.when(mine_ref[0] == side)
            def _():
                for i in range(lead):
                    for j in range(tail):
                        to = i * tail + j
                        for out_ref, which in ((keep_ref, side), (away_ref, 1 - side)):
                            block = (2 * i + which) * tail + j
                            rows = acc_ref[block * part : (block + 1) * part, :]
                            out_ref[to, :part, :] = rows.astype(LOW)
                            out_ref[to, part:, :] = jnp.zeros((fill - part, k), LOW)
                            if extras:
                                values = refs[2 * count][block : block + 1, :]
                                out_ref[to, part : part + 1, : values.shape[1]] = values.astype(LOW)

    rows = sum(left.shape[0] for left in lefts)
    return call(
        kernel,
        (mine.reshape(1),),
        (*lefts, *rights, *extras),
        [array((lead * tail, fill, k)), array((lead * tail, fill, k))],
        scratch=[pltpu.VMEM((dim, k), F32)],
        flops=2 * rows * dim * k,
        after=after,
    )


def swap_blocks(member, keep, got, after=()):
    _, fill, k = keep.shape

    def kernel(member_ref, keep_ref, got_ref, *outs):
        for ref, other in zip(outs, (0, 2, 1, 3)):
            at = member_ref[0] ^ other
            ref[...] = (keep_ref[at].astype(F32) + got_ref[at].astype(F32)).astype(LOW)

    return call(kernel, (member.reshape(1),), (keep, got), [array((fill, k))] * 4, after=after)


def join_feed(member, blocks, part):
    _, hid = blocks[0].shape

    def kernel(member_ref, *refs):
        for who in range(4):

            @pl.when(member_ref[0] == who)
            def _():
                for ref, other in zip(refs, (0, 2, 1, 3)):
                    place = who ^ other
                    refs[-1][:, place * hid : (place + 1) * hid] = ref[:part, :].astype(F32)

    return call(kernel, (member.reshape(1),), blocks, [array((part, 4 * hid), F32)])[0]


def qkv_grad(mp, sources, normed, blocks, part, after=()):
    total, dim = normed.shape
    n, rows, width = blocks.shape[0], blocks.shape[1], blocks.shape[2] // 3
    count = dim // part
    fill = padded(part)

    def kernel(mp_ref, sources_ref, x_ref, in_ref, *refs):
        away_ref, keep_ref, sum_ref, all_ref, acc_ref = refs

        for r in range(n):
            all_ref[r * rows : (r + 1) * rows, :] = in_ref[sources_ref[r]]
        sum_ref[...] = jnp.sum(all_ref[...].astype(F32), axis=0, keepdims=True)
        for start in range(0, dim, 256):
            end = min(start + 256, dim)
            acc_ref[start:end, :] = dot(x_ref[:, start:end], all_ref[...], ((0,), (0,)))
        for side in range(2):

            @pl.when(mp_ref[0] == side)
            def _():
                for i in range(count):
                    at = slice(i * part, (i + 1) * part)
                    keep_ref[i, :part, :] = acc_ref[at, side * width : (side + 2) * width].astype(LOW)
                    away_ref[i, :part, :] = acc_ref[at, (1 - side) * width : (3 - side) * width].astype(LOW)
                    if part < fill:
                        keep_ref[i, part:, :] = jnp.zeros((fill - part, 2 * width), LOW)
                        away_ref[i, part:, :] = jnp.zeros((fill - part, 2 * width), LOW)

    return call(
        kernel,
        (mp.reshape(1), sources),
        (normed, blocks),
        [array((count, fill, 2 * width)), array((count, fill, 2 * width)), array((1, 3 * width), F32)],
        scratch=[pltpu.VMEM((total, 3 * width), LOW), pltpu.VMEM((dim, 3 * width), F32)],
        flops=6 * total * dim * width,
        after=after,
    )


def join_qkv(mp, ctx, spans, received, dim, part, after=()):
    n = len(received)
    fill, double = received[0].shape
    width = double // 2
    n_heads = dim // HD
    cut = dim // 2

    def kernel(mp_ref, ctx_ref, *refs):
        out_ref, in_ref = refs[-2:]
        for i in range(n):
            in_ref[ctx_ref[0] ^ i] = refs[i][...]
        for side in range(2):

            @pl.when(mp_ref[0] == side)
            def _():
                for group in range(n):
                    size, lane = owned(spans, group, n_heads)
                    if not size:
                        continue
                    for first, start in ((0, 0 if side == 0 else -cut), (width, dim if side == 0 else cut)):
                        low = max(start + lane, 0)
                        high = min(start + lane + size, dim + cut)
                        if low < high:
                            source = first + low - start - lane
                            out_ref[:, low:high] = in_ref[group, :part, source : source + high - low].astype(F32)

    return call(
        kernel,
        (mp.reshape(1), ctx.reshape(1)),
        received,
        [array((part, dim + cut), F32)],
        scratch=[pltpu.VMEM((n, fill, double), LOW)],
        after=after,
    )[0]


def pack_late(sums, columns, early, copies, width):
    half, size = sums.shape[1] // 2, early.shape[1]

    def kernel(sums_ref, columns_ref, early_ref, out_ref, row_ref):
        row_ref[...] = jnp.zeros_like(row_ref)
        for i in range(4):
            row_ref[i : i + 1, :] = sums_ref[i // 2 : i // 2 + 1, (i % 2) * half : (i % 2 + 1) * half]
        row_ref[4:6, :size] = early_ref[...]
        row_ref[6:7, :width] = columns_ref[:, :width]
        row_ref[6:7, width : 2 * width] = columns_ref[:, 2 * width :]
        for i in range(copies):
            out_ref[i] = row_ref[...].astype(LOW)

    outs = [array((copies, 8, half))]
    return call(kernel, (), (sums, columns, early), outs, scratch=[pltpu.VMEM((8, half), F32)])[0]


def finish_vectors(mp, late, sizes, spans, dim, hid_half, width, slice_size):
    n_batch, n_ctx, n_mp = sizes
    n_heads = dim // HD
    half = dim // 2
    across = dim // slice_size
    top = n_ctx // 2

    def kernel(mp_ref, in_ref, out_ref, up_ref):
        terms = sum(in_ref[i].astype(F32) for i in range(n_batch * n_ctx * n_mp))
        for i in range(4):
            out_ref[i // 2 : i // 2 + 1, (i % 2) * half : (i % 2 + 1) * half] = terms[i : i + 1, :]

        def total(batch, places, at, size):
            whos = [(batch * n_ctx + place) * n_mp + core for place in places for core in range(n_mp)]
            return sum(in_ref[who].astype(F32)[at : at + 1, :size] for who in whos)

        for group in range(n_ctx):
            size, lane = owned(spans, group, n_heads)
            if not size:
                continue
            value = sum(total(batch, (group,), 6, 2 * width) for batch in range(n_batch))
            out_ref[2:3, lane : lane + size] = value[:, :size]
            out_ref[3:4, lane : lane + size] = value[:, width : width + size]
        early = []
        for i in range(n_batch * n_ctx):
            batch, place = i // n_ctx, i % n_ctx
            early.append(total(batch, (place % top, place % top + top), 4 + place // top, slice_size))
        for i in range(4 * across):
            to = (i % across) * slice_size
            out_ref[4 + i // across : 5 + i // across, to : to + slice_size] = early[i]
        for side in range(n_mp):

            @pl.when(mp_ref[0] == side)
            def _():
                for i in range(hid_half // slice_size):
                    at = 4 * across + side * (hid_half // slice_size) + i
                    up_ref[:, i * slice_size : (i + 1) * slice_size] = early[at]

    results = call(kernel, (mp.reshape(1),), (late,), [array((8, dim), F32), array((1, hid_half), F32)])
    return results[0], results[1].reshape(-1)


def scatter_first(keep, got, rows, after=()):
    dim = keep.shape[1]
    half = rows // 2

    def kernel(keep_ref, got_ref, one_ref, two_ref, own_ref, side_ref):
        def some(first, count):
            return keep_ref[first : first + count, :] + got_ref[first : first + count, :].astype(F32)

        one_ref[...] = some(3 * rows, half).astype(LOW)
        two_ref[...] = some(3 * rows + half, half).astype(LOW)
        own_ref[...] = some(0, rows)
        side_ref[0] = some(rows, rows)
        side_ref[1] = some(2 * rows, rows)

    outs = [array((half, dim)), array((half, dim)), array((rows, dim), F32), array((2, rows, dim), F32)]
    return call(kernel, (), (keep, got), outs, after=after, near=(0, 2, 3, 5))


def scatter_second(side, one, two, after=()):
    _, rows, dim = side.shape
    half = rows // 2

    def kernel(side_ref, one_ref, two_ref, batch_ref, near_ref):
        batch_ref[:half, :] = (side_ref[0, :half, :] + one_ref[...].astype(F32)).astype(LOW)
        batch_ref[half:, :] = side_ref[0, half:, :].astype(LOW)
        near_ref[:half, :] = side_ref[1, :half, :].astype(LOW)
        near_ref[half:, :] = (side_ref[1, half:, :] + two_ref[...].astype(F32)).astype(LOW)

    outs = [array((rows, dim)), array((rows, dim))]
    return call(kernel, (), (side, one, two), outs, after=after, near=(0, 3, 4))


def finish_out(mid, acc, one, two, bias, after=()):
    rows, dim = mid.shape

    def kernel(mid_ref, acc_ref, one_ref, two_ref, bias_ref, out_ref):
        own = acc_ref[...] + one_ref[...].astype(F32) + two_ref[...].astype(F32)
        out_ref[0] = (mid_ref[...] + own + row(bias_ref[...])).T.astype(LOW)

    return call(kernel, (), (mid, acc, one, two, bias), [array((1, dim, rows))], after=after)[0]


def back_out(mp, spans, width, summed, mid, cot, gain, weight):
    acc, one, two = summed
    rows, dim = mid.shape
    n = len(spans)
    cols = dim // 2
    steps = 1
    chunk = dim // steps

    def kernel(mp_ref, acc_ref, one_ref, two_ref, mid_ref, cot_ref, gain_ref, w_ref, *refs):
        _, keep_ref, away_ref, _, outs_ref, low_ref, turned_ref = refs
        step = pl.program_id(0)
        pl.when(step == 0)(functools.partial(first, acc_ref, one_ref, two_ref, mid_ref, cot_ref, gain_ref, refs))
        here = pl.ds(pl.multiple_of(step * chunk, 8), chunk)
        turned_ref[here, :] = dot(w_ref[...], low_ref[...], ((1,), (1,)))

        @pl.when(step == steps - 1)
        def _():
            for group in range(n):
                start = spans[group] * HD
                outs_ref[group] = turned_ref[start : start + width, :].T.astype(LOW)
            for side in range(2):

                @pl.when(mp_ref[0] == side)
                def _():
                    keep_ref[...] = low_ref[:, side * cols : (side + 1) * cols]
                    away_ref[...] = low_ref[:, (1 - side) * cols : (2 - side) * cols]

    def first(acc_ref, one_ref, two_ref, mid_ref, cot_ref, gain_ref, refs):
        grad_ref, _, _, sums_ref, _, low_ref, _ = refs
        full = acc_ref[...] + one_ref[...].astype(F32) + two_ref[...].astype(F32)
        xhat, rstd = norm_parts(mid_ref[...])
        back, gain_grad, shift_grad = norm_back(full, xhat, rstd, row(gain_ref[...]))
        cot_full = cot_ref[0].astype(F32)
        grad = cot_full + back
        grad_ref[...] = grad
        low_ref[...] = grad.astype(LOW)
        sums_ref[0:1, :] = jnp.sum(grad, axis=0, keepdims=True)
        sums_ref[1:2, :] = row(gain_grad)
        sums_ref[2:3, :] = row(shift_grad)
        sums_ref[3:4, :] = jnp.sum(cot_full, axis=0, keepdims=True)

    return call(
        kernel,
        (mp.reshape(1),),
        (acc, one, two, mid, cot, gain, weight),
        [
            array((rows, dim), F32),
            array((rows, cols)),
            array((rows, cols)),
            array((4, dim), F32),
            array((n, rows, width)),
        ],
        scratch=[pltpu.VMEM((rows, dim), LOW), pltpu.VMEM((dim, rows), F32)],
        grid=(steps,),
        in_specs=[None] * 6 + [tall(chunk, dim)],
        flops=2 * rows * dim * dim,
    )


def back_qkv(spans, pieces, weight, tokens, gain, grad_mid, after=()):
    rows, dim = tokens.shape[1:]
    n = len(spans)
    n_heads = dim // HD
    width = pieces.shape[2] // 3
    steps = 5 if dim % 40 == 0 else 1
    chunk = dim // steps

    def kernel(in_ref, w_ref, x_ref, gain_ref, mid_ref, out_ref, vec_ref, all_ref, part_ref):
        step = pl.program_id(0)

        @pl.when(step == 0)
        def _():
            for group in range(n):
                size, lane = owned(spans, group, n_heads)
                for part in range(3 if size else 0):
                    to = part * dim + lane
                    all_ref[:, to : to + size] = in_ref[group, :, part * width : part * width + size]

        part_ref[pl.ds(pl.multiple_of(step * chunk, 8), chunk), :] = dot(w_ref[...], all_ref[...], ((1,), (1,)))

        @pl.when(step == steps - 1)
        def _():
            xhat, rstd = norm_parts(x_ref[0].astype(F32))
            back, gain_grad, shift_grad = norm_back(part_ref[...].T, xhat, rstd, row(gain_ref[...]))
            out_ref[0] = (mid_ref[...] + back).T.astype(LOW)
            vec_ref[0:1, :] = row(gain_grad)
            vec_ref[1:2, :] = row(shift_grad)

    in_specs = [None, tall(chunk, 3 * dim), None, None, None]
    return call(
        kernel,
        (),
        (pieces, weight, tokens, gain, grad_mid),
        [array((1, dim, rows)), array((2, dim), F32)],
        scratch=[
            pltpu.VMEM((rows, 3 * dim), LOW),
            pltpu.VMEM((dim, rows), F32),
        ],
        grid=(steps,),
        in_specs=in_specs,
        flops=6 * rows * dim * dim,
        after=after,
    )


def layer(
    tokens, cotangent, block_table, w_qkv, q_bias, v_bias, w_out, out_bias,
    ln1_gain, ln1_bias, ln2_gain, ln2_bias, w_up, up_bias, w_down, down_bias,
):
    n_ctx, n_mp, n_batch = lax.axis_size(CTX), lax.axis_size(MP), lax.axis_size(BATCH)
    ctx, mp, batch = lax.axis_index(CTX), lax.axis_index(MP), lax.axis_index(BATCH)
    rows, dim = tokens.shape[1], tokens.shape[2]
    total = rows * n_ctx
    SENT.clear()
    GRANT[0] = (36 if total <= 1024 else 60) << 20
    blk = total // block_table.shape[0]
    n_heads = dim // HD
    per = -(-n_heads // n_ctx)
    width = per * HD
    hid_half = w_up.shape[1]
    near = (ctx // NEAR) % 2
    member = batch * 2 + near
    hid = hid_half // (2 * n_batch)
    part = dim // (n_batch * n_ctx)
    half = rows // 2
    spans = [group * (n_heads - per) // (n_ctx - 1) for group in range(n_ctx)]

    ring = ring_of(n_ctx)
    place = [ring.index(i) for i in range(n_ctx)]
    ring_arr = jnp.array(ring, jnp.int32)
    at = jnp.array(place, jnp.int32)[ctx]
    steps = jnp.arange(n_ctx, dtype=jnp.int32)
    sources = ring_arr[(at - steps) % n_ctx]
    blocks_per = rows // blk
    order = block_table.reshape(n_ctx, blocks_per)[sources].reshape(-1)

    starts_of = jnp.array(spans, jnp.int32) * HD
    head_start = starts_of[ctx]
    w_own = jnp.concatenate(
        [lax.dynamic_slice(w_qkv, (0, head_start + i * dim), (dim, width)) for i in range(3)], axis=1
    )
    bias_own = jnp.concatenate(
        [
            lax.dynamic_slice(q_bias, (head_start,), (width,)),
            jnp.zeros((width,), F32),
            lax.dynamic_slice(v_bias, (head_start,), (width,)),
        ]
    )

    def gather_first(own, own_near, far):
        return flip(own, BATCH, 1, far), flip(own_near, CTX, NEAR, far)

    def gather_second(sides, far):
        return flip(sides[0][:half], CTX, NEAR, far), flip(sides[1][half:], BATCH, 1, far)

    def exchange(blocks):
        return sent(lax.all_to_all(blocks, CTX, split_axis=0, concat_axis=0, tiled=True))

    tokens, normed_one = norm_in(tokens.transpose(0, 2, 1), ln1_gain, ln1_bias)
    normed_pieces = ring_gather(normed_one, ring)
    w_down_own = lax.dynamic_slice(w_down.T, (0, member * hid), (dim, hid))
    up_bias_own = lax.dynamic_slice(up_bias, (member * hid,), (hid,))
    qkv, normed_all = project_qkv(order, normed_pieces, w_own, row(bias_own), blk, (w_down_own, up_bias_own))

    cot_own = cotangent[0]
    cot_near, _ = lax.optimization_barrier((cot_own, normed_pieces[n_ctx // 2]))
    cot_sides = gather_first(cot_own, cot_near, True)
    attn_heads, lse = attn_forward(order, sources, qkv, rows, blk)
    attn_pieces = exchange(attn_heads)
    cot_chip = pack([cot_own, *cot_sides, *gather_second(cot_sides, True)], (lse,))
    cot_groups = cot_chip, flip(cot_chip, MP, 1)
    attn_rows, resid_mid, normed_two = project_out(
        spans, attn_pieces, w_out, tokens, (out_bias, ln2_gain, ln2_bias), (cot_chip,)
    )

    near_rows = gather_first(normed_two, normed_two, False)
    far_rows = gather_second(near_rows, False)
    w_up_later, _ = lax.optimization_barrier((w_up, normed_two))
    w_up_own = lax.dynamic_slice(w_up_later, (0, member * hid), (dim, hid))
    hidden_back_keep = feed_dot(cot_groups[0], w_down_own, False, F32, (normed_two,))
    normed_chip = pack([normed_two, *near_rows, *far_rows], (hidden_back_keep,))
    normed_groups = normed_chip, flip(normed_chip, MP, 1)
    hidden_back_away = feed_dot(cot_groups[1], w_down_own, False, F32, (normed_chip,), (1, 2))
    hidden_away, low_away, back_away, sum_away = feed(
        normed_groups[1], w_up_own, up_bias_own, hidden_back_away, LOW, (), (1, 3, 6)
    )
    hidden_keep, low_keep, back_keep, sum_keep = feed(
        normed_groups[0], w_up_own, up_bias_own, hidden_back_keep, F32, (back_away,), (1, 6)
    )
    one, two, acc, side = scatter_first(back_keep, flip(back_away, MP, 1), rows)
    one_got, two_got = flip(one, CTX, NEAR), flip(two, BATCH, 1)
    by_batch, by_near = scatter_second(side, one_got, two_got)
    down_away = feed_dot(hidden_away, w_down_own, True, LOW, (by_near,))
    grad_normed_two = acc, flip(by_batch, BATCH, 1), flip(by_near, CTX, NEAR)
    up_shift_grad = (sum_keep + sum_away).reshape(-1)

    grad_mid, mid_keep, mid_away, mid_vectors, by_group = back_out(
        mp, spans, width, grad_normed_two, resid_mid, cotangent, ln2_gain, w_out
    )
    grad_heads = exchange(by_group)

    bits = []
    bit = 1
    while bit < n_ctx:
        bits.append(bit)
        bit *= 2

    def feed_grad(lefts, rights, after):
        away, keep = weight_grad(ctx % 2, lefts, rights, part, (n_batch * n_ctx // 2, 1), after)
        return flip(away, CTX, 1), keep

    def feed_half(got, keep, after=()):
        left = [bit for bit in reversed(bits) if bit > 1]
        halves = [bit for bit in bits if bit > 1 and bit != NEAR]
        first = None
        for bit in halves:
            lead = n_batch * 2 ** left.index(bit)
            tail = 2 ** (len(left) - 1 - left.index(bit))
            away, keep = halve((ctx // bit) % 2, keep, got, (lead, tail), after if first is None else ())
            first = away if first is None else first
            got = flip(away, CTX, bit)
            left.remove(bit)
        return first, got, keep

    def feed_swap(got, keep, after=()):
        mine, to_batch, to_near, to_both = swap_blocks(member, keep, got, after)
        pairs = [(b * n_ctx + c, (1 - b) * n_ctx + (c ^ NEAR)) for b in range(n_batch) for c in range(n_ctx)]
        both = permute(to_both, (BATCH, CTX), pairs)
        far, got = flip(to_batch, BATCH, 1), flip(to_near, CTX, NEAR)
        return mine, (mine, far, got, both)

    down_got, down_kept = feed_grad(cot_groups, (hidden_keep, hidden_away), (one,))


    everyone = (BATCH, CTX, MP)
    n_all = n_batch * n_ctx * n_mp
    early = jnp.concatenate(
        [
            mid_vectors.reshape(-1),
            lax.dynamic_update_slice(
                jnp.zeros((hid_half * n_mp,), F32), up_shift_grad, (mp * hid_half + member * hid,)
            ),
        ]
    ).reshape(n_batch * n_ctx, -1)
    out_away, out_kept = weight_grad(
        batch, (attn_rows, flip(attn_rows, MP)), (mid_keep, flip(mid_away, MP)), part, (1, n_ctx), (grad_mid,), early
    )
    out_got = flip(out_away, BATCH, 1)
    up_got, up_kept = feed_grad(normed_groups, (low_keep, low_away), (out_kept,))
    down_first, down_got, down_kept = feed_half(down_got, down_kept, (up_kept,))
    out_bits = [NEAR] + [bit for bit in bits if bit != NEAR]
    left = bits[::-1]

    def out_half(level, out_got, out_kept, after=(), extra=0):
        bit = out_bits[level]
        lead, tail = 2 ** left.index(bit), 2 ** (len(left) - 1 - left.index(bit))
        left.remove(bit)
        away, keep, *rest = halve((ctx // bit) % 2, out_kept, out_got, (lead, tail), after, part, extra)
        return (away, flip(away, CTX, bit), keep, *rest)


    grad_blocks = attn_backward(order, sources, qkv, grad_heads, attn_heads, lse, rows, blk, (down_first,))
    pieces_back = exchange(grad_blocks)


    qkv_away, qkv_kept, column_sums = qkv_grad(mp, sources, normed_all, grad_blocks, part)
    qkv_got = flip(qkv_away, MP, 1)
    out_first, out_got, out_kept = out_half(0, out_got, out_kept, (qkv_kept,))
    qkv_away, qkv_kept = halve(batch, qkv_kept, qkv_got, (1, n_ctx), (out_first,))
    qkv_got = flip(qkv_away, BATCH, 1)
    up_first, up_got, up_kept = feed_half(up_got, up_kept, (qkv_kept,))

    down_keep = feed_dot(hidden_keep, w_down_own, True, F32, (up_first,))
    last, other, last_acc, last_side = scatter_first(down_keep, flip(down_away, MP), rows)
    last_got, other_got = flip(last, CTX, NEAR), flip(other, BATCH, 1)
    down_swap, down_parts = feed_swap(down_got, down_kept, (last,))
    values = add_blocks(ctx, qkv_kept, qkv_got, (down_swap,))
    received = [values[0]] + [flip(values[i], CTX, i) for i in range(1, n_ctx)]
    for level in range(1, len(bits) - 1):
        out_first, out_got, out_kept = out_half(level, out_got, out_kept, (values[0],))
    tokens_grad_rows, in_vectors = back_qkv(
        spans, pieces_back, w_qkv, tokens, ln1_gain, grad_mid, (out_first,)
    )
    out_first, out_got, out_kept, early_sum = out_half(
        len(bits) - 1, out_got, out_kept, (in_vectors,), early.shape[1]
    )
    late = pack_late(in_vectors, column_sums, early_sum, n_all, width)
    packed = late
    late, _ = lax.optimization_barrier((late, pieces_back))
    late = lax.all_to_all(late, everyone, split_axis=0, concat_axis=0, tiled=True)
    vector_sum, up_bias_grad = finish_vectors(
        mp, late, (n_batch, n_ctx, n_mp), spans, dim, hid_half, width, early.shape[1]
    )
    last_batch, last_near = scatter_second(last_side, last_got, other_got, (packed,))
    last_sides = flip(last_batch, BATCH, 1), flip(last_near, CTX, NEAR)
    down_part = join_feed(member, down_parts, part).T
    qkv_part = join_qkv(mp, ctx, spans, received, dim, part, (last_near,))
    out_value = join_out(out_kept, out_got, part, (qkv_part,))
    up_swap, up_parts = feed_swap(up_got, up_kept, (out_value,))
    layer_rows = finish_out(resid_mid, last_acc, *last_sides, down_bias, (up_swap,))
    up_part = join_feed(member, up_parts, part)
    return (
        layer_rows.transpose(0, 2, 1),
        tokens_grad_rows.transpose(0, 2, 1),
        qkv_part,
        out_value,
        up_part,
        down_part,
        up_bias_grad,
        vector_sum,
    )


def solution(mesh):
    return jax.shard_map(
        layer,
        mesh=mesh,
        in_specs=(
            P((BATCH, MP), CTX, None),
            P((BATCH, MP), CTX, None),
            P(),
            P(),
            P(),
            P(),
            P(),
            P(),
            P(),
            P(),
            P(),
            P(),
            P(None, MP),
            P(MP),
            P(MP, None),
            P(),
        ),
        out_specs=(
            P((BATCH, MP), CTX, None),
            P((BATCH, MP), CTX, None),
            P((BATCH, CTX), MP),
            P((BATCH, CTX), MP),
            P((BATCH, CTX), MP),
            P(MP, (BATCH, CTX)),
            P(MP),
            P(),
        ),
        check_vma=False,
    )
```

```python
import functools


import jax
import jax.numpy as jnp
from jax import lax
from jax.experimental import pallas as pl
from jax.experimental.pallas import tpu as pltpu
from jax.sharding import PartitionSpec as P

HD = 64
NORM_EPSILON = 1e-05
MASKED_SCORE = -1e30
GELU_C = 0.7978845608028654
GELU_A = 0.044715
LOW = jnp.bfloat16
BATCH, CTX, MP = "batch", "ctx", "mp"
F32 = jnp.float32
NEAR = 2


def norm_parts(rows):
    mean = jnp.mean(rows, axis=-1, keepdims=True)
    centered = rows - mean
    var = jnp.mean(centered * centered, axis=-1, keepdims=True)
    rstd = lax.rsqrt(var + NORM_EPSILON)
    return centered * rstd, rstd


def norm_back(grad, xhat, rstd, gain):
    scaled = grad * gain
    mean_one = jnp.mean(scaled, axis=-1, keepdims=True)
    mean_two = jnp.mean(scaled * xhat, axis=-1, keepdims=True)
    rows = rstd * (scaled - mean_one - xhat * mean_two)
    return rows, jnp.sum(grad * xhat, axis=0), jnp.sum(grad, axis=0)


def dot(left, right, dims):
    return lax.dot_general(left, right, (dims, ((), ())), preferred_element_type=F32)


SENT = {}
KEPT = {}


def sent(value):
    SENT[id(value)] = value
    return value


def permute(value, axis, pairs, far=False):
    shape = value.shape
    if shape[-2] % 8 == 0:
        value = value.reshape((*shape[:-2], shape[-2] // 8, 8, shape[-1]))
    value = lax.ppermute(value, axis, pairs).reshape(shape)
    return value if far else sent(value)


def flip(value, axis, bit=1, far=False):
    size = lax.axis_size(axis)
    return permute(value, axis, [(i, i ^ bit) for i in range(size)], far)


def ring_of(size):
    evens = list(range(0, size, 2))
    odds = list(range(1, size, 2))
    return evens + odds[::-1]


def shift(value, ring, step):
    size = len(ring)
    return permute(value, CTX, [(ring[i], ring[(i + step) % size]) for i in range(size)], True)


def ring_gather(own, ring):
    size = len(ring)
    half = size // 2
    ahead, behind = own, own
    blocks = [None] * size
    blocks[0] = [own]
    for step in range(1, half):
        ahead = shift(ahead, ring, 1)
        behind = shift(behind, ring, -1)
        blocks[step] = [ahead]
        blocks[size - step] = [behind]
    cut = own.shape[0] // 2
    blocks[half] = [shift(ahead[:cut], ring, 1), shift(behind[cut:], ring, -1)]
    return [piece for block in blocks for piece in block]


GRANT = [0]


def call(
    kernel, scalars, args, outs, scratch=(), grid=(1,), in_specs=None, out_specs=None, flops=0, exps=0, after=(), near=()
):
    def whole(shape):
        return pl.BlockSpec(shape, lambda *_: (0,) * len(shape))

    in_specs = in_specs or [None] * len(args)
    out_specs = out_specs or [None] * len(outs)
    in_specs = [spec or whole(arg.shape) for spec, arg in zip(in_specs, args)]
    out_specs = [spec or whole(out.shape) for spec, out in zip(out_specs, outs)]
    moved = sum(a.size * a.dtype.itemsize for a in (*args, *outs))
    args = tuple(
        arg
        if i in near or arg.size < 4096 or id(arg) in SENT
        else pltpu.with_memory_space_constraint(arg, pltpu.HBM)
        for i, arg in enumerate(args)
    )
    shapes = [
        out if len(args) + i in near or out.size < 4096 else pltpu.HBM(out.shape, out.dtype)
        for i, out in enumerate(outs)
    ]
    if after:
        inner, first = kernel, len(scalars) + len(args)
        in_specs = in_specs + [pl.BlockSpec(memory_space=pl.ANY)] * len(after)

        def kernel(*refs):
            inner(*refs[:first], *refs[first + len(after) :])

    after = tuple(pltpu.with_memory_space_constraint(a, pltpu.HBM) if id(a) in KEPT else a for a in after)
    results = pl.pallas_call(
        kernel,
        grid_spec=pltpu.PrefetchScalarGridSpec(
            num_scalar_prefetch=len(scalars),
            grid=grid,
            in_specs=in_specs,
            out_specs=out_specs,
            scratch_shapes=list(scratch),
        ),
        out_shape=shapes,
        compiler_params=pltpu.CompilerParams(vmem_limit_bytes=GRANT[0]),
        cost_estimate=pl.CostEstimate(flops=flops, transcendentals=exps, bytes_accessed=moved),
    )(*scalars, *args, *after)
    for i, (out, result) in enumerate(zip(outs, results)):
        if len(args) + i not in near and out.size >= 4096:
            KEPT[id(result)] = result
    return results


def tall(tile, width):
    return pl.BlockSpec((tile, width), lambda i, *_: (i, 0))


def tile_of(rows, most=256):
    return most if rows % most == 0 else rows


def array(shape, dtype=LOW):
    return jax.ShapeDtypeStruct(shape, dtype)


def row(vector):
    return vector[None, :]


def norm_in(turned, gain, shift_by):
    _, dim, rows = turned.shape

    def kernel(x_ref, gain_ref, shift_ref, rows_ref, o_ref):
        value = x_ref[0].astype(F32).T
        rows_ref[0] = value.astype(LOW)
        xhat, _ = norm_parts(value)
        o_ref[...] = (xhat * row(gain_ref[...]) + row(shift_ref[...])).astype(LOW)

    return call(kernel, (), (turned, gain, shift_by), [array((1, rows, dim)), array((rows, dim))])


def pack(pieces, after=()):
    def kernel(*refs):
        at = 0
        for ref in refs[:-1]:
            refs[-1][at : at + ref.shape[0], :] = ref[...]
            at += ref.shape[0]

    rows = sum(piece.shape[0] for piece in pieces)
    return call(kernel, (), pieces, [array((rows, pieces[0].shape[1]))], after=after)[0]


def project_qkv(order, pieces, weight, bias, blk, after=()):
    total = sum(piece.shape[0] for piece in pieces)
    width = weight.shape[1]

    def kernel(order_ref, *refs):
        ins, (w_ref, b_ref, qkv_ref, all_ref) = refs[: len(pieces)], refs[len(pieces) :]
        at = 0
        for ref in ins:
            all_ref[at : at + ref.shape[0], :] = ref[...]
            at += ref.shape[0]
        step = min(512, total)
        for start in range(0, total, step):
            out = dot(all_ref[start : start + step, :], w_ref[...], ((1,), (0,))) + b_ref[...]
            for part in range(step // blk):
                to = pl.multiple_of(order_ref[start // blk + part] * blk, blk)
                qkv_ref[pl.ds(to, blk), :] = out[part * blk : (part + 1) * blk].astype(LOW)

    return call(
        kernel,
        (order,),
        (*pieces, weight, bias),
        [array((total, width)), array((total, weight.shape[0]))],
        flops=2 * total * width * weight.shape[0],
        after=after,
    )


def lanes_of(shape, axis, head):
    lane = lax.broadcasted_iota(jnp.int32, shape, axis)
    return (lane >= head * HD) & (lane < (head + 1) * HD)


def attn_sizes(rows, width):
    heads = 2 if (width // HD) % 2 == 0 else 1
    block = heads * HD
    tile = min(512, rows)
    return heads, block, width // block, tile, rows // tile


def for_tiles(tile, tiles, body):
    if tiles > 4:
        body(tile * tiles)
        return
    for t in range(tiles):
        pl.when(pl.program_id(1) == t)(functools.partial(body, (t + 1) * tile))


def lanes_at(base, group, block, groups):
    if groups == 1:
        return slice(base, base + block)
    return pl.ds(pl.multiple_of(base + group * block, block), block)


def masked(scores, fill, tiles):
    keys, tile = scores.shape
    first = 0 if tiles > 4 else keys - tile
    key = lax.broadcasted_iota(jnp.int32, (keys - first, tile), 0) + first
    query = lax.broadcasted_iota(jnp.int32, (keys - first, tile), 1) + pl.program_id(1) * tile
    last = jnp.where(key <= query, scores[first:], fill)
    return jnp.concatenate([scores[:first], last], axis=0) if first else last


def attn_forward(order, sources, qkv, rows, blk, after=()):
    total, width = qkv.shape[0], qkv.shape[1] // 3
    heads, block, groups, tile, tiles = attn_sizes(total, width)
    n = total // rows
    per = rows // blk

    def kernel(order_ref, sources_ref, qkv_ref, *refs):
        outs_ref, lse_ref, sorted_ref = refs[0], refs[-2], refs[-1]
        group, t = pl.program_id(0), pl.program_id(1)
        at = lanes_at(0, group, block, groups)
        first = pl.multiple_of(t * tile, tile)
        queries = qkv_ref[pl.ds(first, tile), at] * LOW(HD**-0.5)

        def body(keys_seen):
            keys = qkv_ref[:keys_seen, lanes_at(width, group, block, groups)]
            values = qkv_ref[:keys_seen, lanes_at(2 * width, group, block, groups)]
            total_out = None
            for head in range(heads):
                part = jnp.where(lanes_of(queries.shape, 1, head), queries, LOW(0))
                scores = masked(dot(keys, part, ((1,), (1,))), MASKED_SCORE, tiles)
                top = jnp.max(scores, axis=0, keepdims=True)
                weights = jnp.exp(scores - top)
                mass = jnp.sum(weights, axis=0, keepdims=True)
                lse_ref[group, t, head : head + 1, :] = top + jnp.log(mass)
                out = dot(values, weights.astype(LOW), ((0,), (0,))) * (1.0 / mass)
                total_out = out if head == 0 else jnp.where(lanes_of(out.shape, 0, head), out, total_out)
            sorted_ref[pl.ds(first, tile), at] = total_out.T.astype(LOW)

        for_tiles(tile, tiles, body)

        @pl.when((group == groups - 1) & (t == tiles - 1))
        def _():
            for r in range(n):
                for i in range(per):
                    source = pl.multiple_of(order_ref[r * per + i] * blk, blk)
                    outs_ref[sources_ref[r], i * blk : (i + 1) * blk, :] = sorted_ref[pl.ds(source, blk), :]

    results = call(
        kernel,
        (order, sources),
        (qkv,),
        [array((n, rows, width)), array((groups, tiles, heads, tile), F32)],
        scratch=[pltpu.VMEM((total, width), LOW)],
        grid=(groups, tiles),
        flops=4 * total * total * width,
        exps=total * total * width // HD,
        after=after,
    )
    return results


def attn_backward(order, sources, ranks, ctx, qkv, grads, outs, lse, rows, blk, after=()):
    total, width = qkv.shape[0], qkv.shape[1] // 3
    heads, block, groups, tile, tiles = attn_sizes(total, width)
    n = total // rows
    per = rows // blk

    def kernel(order_ref, sources_ref, ranks_ref, ctx_ref, qkv_ref, lse_ref, g_ref, o_ref, *refs):
        d_refs = refs[:n]
        g_all, o_all, dq_all, k_acc, v_acc, d_all = refs[n:]
        group, t = pl.program_id(0), pl.program_id(1)
        at = lanes_at(0, group, block, groups)
        first = pl.multiple_of(t * tile, tile)

        @pl.when((group == 0) & (t == 0))
        def _():
            for r in range(n):
                for i in range(per):
                    to = pl.multiple_of(order_ref[r * per + i] * blk, blk)
                    g_all[pl.ds(to, blk), :] = g_ref[sources_ref[r], i * blk : (i + 1) * blk, :]
                    o_all[pl.ds(to, blk), :] = o_ref[sources_ref[r], i * blk : (i + 1) * blk, :]

        @pl.when(t == 0)
        def _():
            k_acc[...] = jnp.zeros_like(k_acc)
            v_acc[...] = jnp.zeros_like(v_acc)

        queries = qkv_ref[pl.ds(first, tile), at] * LOW(HD**-0.5)
        grads_here = g_all[pl.ds(first, tile), at]
        product = (grads_here.astype(F32) * o_all[pl.ds(first, tile), at].astype(F32)).T

        def body(seen):
            keys = qkv_ref[:seen, lanes_at(width, group, block, groups)]
            values = qkv_ref[:seen, lanes_at(2 * width, group, block, groups)]
            total_out = None
            for head in range(heads):
                pick = lanes_of(queries.shape, 1, head)
                part = jnp.where(pick, queries, LOW(0))
                grad = jnp.where(pick, grads_here, LOW(0))
                delta = jnp.sum(product[head * HD : (head + 1) * HD, :], axis=0, keepdims=True)
                scores = dot(keys, part, ((1,), (1,)))
                probs = masked(jnp.exp(scores - lse_ref[group, t, head : head + 1, :]), 0.0, tiles)
                back = dot(values, grad, ((1,), (1,)))
                inner = (probs * (back - delta)).astype(LOW)
                v_acc[:seen, :] += dot(probs.astype(LOW), grad, ((1,), (0,)))
                k_acc[:seen, :] += dot(inner, part, ((1,), (0,)))
                out = dot(keys, inner, ((0,), (0,)))
                total_out = out if head == 0 else jnp.where(lanes_of(out.shape, 0, head), out, total_out)
            dq_all[pl.ds(first, tile), :] = (total_out * (HD**-0.5)).T

        for_tiles(tile, tiles, body)

        @pl.when(t == tiles - 1)
        def _():
            for part, ref in enumerate((dq_all, k_acc, v_acc)):
                d_all[:, lanes_at(part * width, group, block, groups)] = ref[...].astype(LOW)

        @pl.when((group == groups - 1) & (t == tiles - 1))
        def _():
            for other in range(n):
                rank = ranks_ref[ctx_ref[0] ^ other]
                for i in range(per):
                    source = pl.multiple_of(order_ref[rank * per + i] * blk, blk)
                    d_refs[other][i * blk : (i + 1) * blk, :] = d_all[pl.ds(source, blk), :]

    return call(
        kernel,
        (order, sources, ranks, ctx.reshape(1)),
        (qkv, lse, grads, outs),
        [array((rows, 3 * width))] * n,
        scratch=[
            pltpu.VMEM((total, width), LOW),
            pltpu.VMEM((total, width), LOW),
            pltpu.VMEM((total, block), F32),
            pltpu.VMEM((total, block), F32),
            pltpu.VMEM((total, block), F32),
            pltpu.VMEM((total, 3 * width), LOW),
        ],
        grid=(groups, tiles),
        flops=10 * total * total * width,
        exps=total * total * width // HD,
        after=after,
    )


def owned(spans, group, n_heads):
    low = spans[group]
    high = spans[group + 1] if group + 1 < len(spans) else n_heads
    return (high - low) * HD, low * HD


def project_out(spans, pieces, weight, tokens, vectors, after=()):
    rows, dim = tokens.shape[1:]
    n = len(spans)
    n_heads = dim // HD

    def kernel(in_ref, w_ref, x_ref, bias_ref, gain_ref, shift_ref, attn_ref, mid_ref, normed_ref):
        for group in range(n):
            size, lane = owned(spans, group, n_heads)
            if size:
                attn_ref[:, lane : lane + size] = in_ref[group, :, :size]
        mid = x_ref[0].astype(F32) + dot(attn_ref[...], w_ref[...], ((1,), (0,)))
        mid = mid + row(bias_ref[...])
        mid_ref[...] = mid
        xhat, _ = norm_parts(mid)
        normed_ref[...] = (xhat * row(gain_ref[...]) + row(shift_ref[...])).astype(LOW)

    return call(
        kernel,
        (),
        (pieces, weight, tokens, *vectors),
        [array((rows, dim)), array((rows, dim), F32), array((rows, dim))],
        flops=2 * rows * dim * dim,
        after=after,
    )


def feed(normed, weight, bias, grad_hidden, out_dtype, after=(), near=()):
    rows, dim = normed.shape
    hid = weight.shape[1]
    tile = tile_of(rows)

    def kernel(x_ref, w_ref, b_ref, gh_ref, hidden_ref, grad_ref, out_ref, sum_ref):
        @pl.when(pl.program_id(0) == 0)
        def _():
            sum_ref[...] = jnp.zeros_like(sum_ref)

        v = dot(x_ref[...], w_ref[...], ((1,), (0,))) + row(b_ref[...])
        square = v * v
        tanh = jnp.tanh(GELU_C * (v + GELU_A * (square * v)))
        half_one = 0.5 * (1.0 + tanh)
        hidden_ref[...] = (v * half_one).astype(LOW)
        slope = half_one + 0.5 * v * (1.0 - tanh * tanh) * GELU_C * (1.0 + 3.0 * GELU_A * square)
        grad = gh_ref[...] * slope
        grad_ref[...] = grad.astype(LOW)
        sum_ref[...] += jnp.sum(grad, axis=0, keepdims=True)
        out_ref[...] = dot(grad_ref[...], w_ref[...], ((1,), (1,))).astype(out_dtype)

    return call(
        kernel,
        (),
        (normed, weight, bias, grad_hidden),
        [array((rows, hid)), array((rows, hid)), array((rows, dim), out_dtype), array((1, hid), F32)],
        grid=(rows // tile,),
        in_specs=[tall(tile, dim), None, None, tall(tile, hid)],
        out_specs=[tall(tile, hid), tall(tile, hid), tall(tile, dim), None],
        flops=4 * rows * dim * hid,
        exps=rows * hid,
        after=after,
        near=near,
    )


def feed_dot(left, right, turned, out_dtype, after=(), near=(1,)):
    rows, width = left.shape[0], right.shape[0 if turned else 1]

    def kernel(x_ref, w_ref, out_ref):
        dims = ((1,), (1,)) if turned else ((1,), (0,))
        out_ref[...] = dot(x_ref[...], w_ref[...], dims).astype(out_dtype)

    tile = tile_of(rows)
    return call(
        kernel,
        (),
        (left, right),
        [array((rows, width), out_dtype)],
        grid=(rows // tile,),
        in_specs=[tall(tile, left.shape[1]), None],
        out_specs=[tall(tile, width)],
        flops=2 * left.size * width,
        after=after,
        near=near,
    )[0]


def halve(mine, keep, got, splits, after=(), part=0, extra=0):
    lead, tail = splits
    _, fill, k = keep.shape

    def kernel(mine_ref, keep_ref, got_ref, away_ref, out_ref, *extra_refs):
        for i in range(lead):
            stay = (2 * i + mine_ref[0]) * tail
            go = (2 * i + 1 - mine_ref[0]) * tail
            for j in range(tail):
                away_ref[i * tail + j] = (keep_ref[go + j].astype(F32) + got_ref[go + j].astype(F32)).astype(LOW)
                out_ref[i * tail + j] = (keep_ref[stay + j].astype(F32) + got_ref[stay + j].astype(F32)).astype(LOW)
        for ref in extra_refs:
            for i in range(2 * lead * tail):
                row_of = keep_ref[i, part : part + 1, :].astype(F32) + got_ref[i, part : part + 1, :].astype(F32)
                ref[i : i + 1, :] = row_of[:, :extra]

    outs = [array((lead * tail, fill, k)), array((lead * tail, fill, k))]
    if extra:
        outs.append(array((2 * lead * tail, extra), F32))
    return call(kernel, (mine.reshape(1),), (keep, got), outs, after=after)


def add_blocks(ctx, keep, got, after=()):
    blocks, fill, k = keep.shape

    def kernel(ctx_ref, keep_ref, got_ref, *outs):
        for i in range(blocks):
            at = ctx_ref[0] ^ i
            outs[i][...] = (keep_ref[at].astype(F32) + got_ref[at].astype(F32)).astype(LOW)

    return call(kernel, (ctx.reshape(1),), (keep, got), [array((fill, k))] * blocks, after=after)


def join_out(keep, got, part, after=()):
    _, _, k = keep.shape

    def kernel(keep_ref, got_ref, out_ref):
        out_ref[...] = keep_ref[0, :part, :].astype(F32) + got_ref[0, :part, :].astype(F32)

    return call(kernel, (), (keep, got), [array((part, k), F32)], after=after)[0]


def padded(part):
    return (part // 8 + 1) * 8


def weight_grad(mine, lefts, rights, part, splits, after=(), extra=None):
    fill = padded(part)
    dim, k = lefts[0].shape[1], rights[0].shape[1]
    lead, tail = splits
    count = len(lefts)
    extras = () if extra is None else (extra,)

    def kernel(mine_ref, *refs):
        ls, rs = refs[:count], refs[count : 2 * count]
        away_ref, keep_ref, acc_ref = refs[-3:]
        step = 256
        for at in range(0, dim, step):
            end = min(at + step, dim)
            value = dot(ls[0][:, at:end], rs[0][...], ((0,), (0,)))
            for left, right in zip(ls[1:], rs[1:]):
                value += dot(left[:, at:end], right[...], ((0,), (0,)))
            acc_ref[at:end, :] = value
        for side in range(2):

            @pl.when(mine_ref[0] == side)
            def _():
                for i in range(lead):
                    for j in range(tail):
                        to = i * tail + j
                        for out_ref, which in ((keep_ref, side), (away_ref, 1 - side)):
                            block = (2 * i + which) * tail + j
                            rows = acc_ref[block * part : (block + 1) * part, :]
                            out_ref[to, :part, :] = rows.astype(LOW)
                            out_ref[to, part:, :] = jnp.zeros((fill - part, k), LOW)
                            if extras:
                                values = refs[2 * count][block : block + 1, :]
                                out_ref[to, part : part + 1, : values.shape[1]] = values.astype(LOW)

    rows = sum(left.shape[0] for left in lefts)
    return call(
        kernel,
        (mine.reshape(1),),
        (*lefts, *rights, *extras),
        [array((lead * tail, fill, k)), array((lead * tail, fill, k))],
        scratch=[pltpu.VMEM((dim, k), F32)],
        flops=2 * rows * dim * k,
        after=after,
    )


def swap_blocks(member, keep, got, after=()):
    _, fill, k = keep.shape

    def kernel(member_ref, keep_ref, got_ref, *outs):
        for ref, other in zip(outs, (0, 2, 1, 3)):
            at = member_ref[0] ^ other
            ref[...] = (keep_ref[at].astype(F32) + got_ref[at].astype(F32)).astype(LOW)

    return call(kernel, (member.reshape(1),), (keep, got), [array((fill, k))] * 4, after=after)


def join_feed(member, blocks, part, after=()):
    _, hid = blocks[0].shape

    def kernel(member_ref, *refs):
        for who in range(4):

            @pl.when(member_ref[0] == who)
            def _():
                for ref, other in zip(refs, (0, 2, 1, 3)):
                    place = who ^ other
                    refs[-1][:, place * hid : (place + 1) * hid] = ref[:part, :].astype(F32)

    return call(kernel, (member.reshape(1),), blocks, [array((part, 4 * hid), F32)], after=after)[0]


def qkv_grad(mp, ranks, ctx, normed, pieces, part, after=()):
    total, dim = normed.shape
    n, rows, width = len(pieces), pieces[0].shape[0], pieces[0].shape[1] // 3
    count = dim // part
    fill = padded(part)

    def kernel(mp_ref, ranks_ref, ctx_ref, x_ref, *refs):
        away_ref, keep_ref, sum_ref, all_ref, acc_ref = refs[n:]
        for other in range(n):
            to = pl.multiple_of(ranks_ref[ctx_ref[0] ^ other] * rows, rows)
            all_ref[pl.ds(to, rows), :] = refs[other][...]
        sum_ref[...] = jnp.sum(all_ref[...].astype(F32), axis=0, keepdims=True)
        for start in range(0, dim, 256):
            end = min(start + 256, dim)
            acc_ref[start:end, :] = dot(x_ref[:, start:end], all_ref[...], ((0,), (0,)))
        for side in range(2):

            @pl.when(mp_ref[0] == side)
            def _():
                for i in range(count):
                    at = slice(i * part, (i + 1) * part)
                    keep_ref[i, :part, :] = acc_ref[at, side * width : (side + 2) * width].astype(LOW)
                    away_ref[i, :part, :] = acc_ref[at, (1 - side) * width : (3 - side) * width].astype(LOW)
                    if part < fill:
                        keep_ref[i, part:, :] = jnp.zeros((fill - part, 2 * width), LOW)
                        away_ref[i, part:, :] = jnp.zeros((fill - part, 2 * width), LOW)

    return call(
        kernel,
        (mp.reshape(1), ranks, ctx.reshape(1)),
        (normed, *pieces),
        [array((count, fill, 2 * width)), array((count, fill, 2 * width)), array((1, 3 * width), F32)],
        scratch=[pltpu.VMEM((total, 3 * width), LOW), pltpu.VMEM((dim, 3 * width), F32)],
        flops=6 * total * dim * width,
        after=after,
    )


def join_qkv(mp, ctx, spans, received, dim, part, after=()):
    n = len(received)
    fill, double = received[0].shape
    width = double // 2
    n_heads = dim // HD
    cut = dim // 2

    def kernel(mp_ref, ctx_ref, *refs):
        out_ref, in_ref = refs[-2:]
        for i in range(n):
            in_ref[ctx_ref[0] ^ i] = refs[i][...]
        for side in range(2):

            @pl.when(mp_ref[0] == side)
            def _():
                for group in range(n):
                    size, lane = owned(spans, group, n_heads)
                    if not size:
                        continue
                    for first, start in ((0, 0 if side == 0 else -cut), (width, dim if side == 0 else cut)):
                        low = max(start + lane, 0)
                        high = min(start + lane + size, dim + cut)
                        if low < high:
                            source = first + low - start - lane
                            out_ref[:, low:high] = in_ref[group, :part, source : source + high - low].astype(F32)

    return call(
        kernel,
        (mp.reshape(1), ctx.reshape(1)),
        received,
        [array((part, dim + cut), F32)],
        scratch=[pltpu.VMEM((n, fill, double), LOW)],
        after=after,
    )[0]


def pack_late(sums, columns, early, copies, width):
    half, size = sums.shape[1] // 2, early.shape[1]

    def kernel(sums_ref, columns_ref, early_ref, out_ref, row_ref):
        row_ref[...] = jnp.zeros_like(row_ref)
        for i in range(4):
            row_ref[i : i + 1, :] = sums_ref[i // 2 : i // 2 + 1, (i % 2) * half : (i % 2 + 1) * half]
        row_ref[4:6, :size] = early_ref[...]
        row_ref[6:7, :width] = columns_ref[:, :width]
        row_ref[6:7, width : 2 * width] = columns_ref[:, 2 * width :]
        for i in range(copies):
            out_ref[i] = row_ref[...].astype(LOW)

    outs = [array((copies, 8, half))]
    return call(kernel, (), (sums, columns, early), outs, scratch=[pltpu.VMEM((8, half), F32)])[0]


def finish_vectors(mp, late, sizes, spans, dim, hid_half, width, slice_size):
    n_batch, n_ctx, n_mp = sizes
    n_heads = dim // HD
    half = dim // 2
    across = dim // slice_size
    top = n_ctx // 2

    def kernel(mp_ref, in_ref, out_ref, up_ref):
        terms = sum(in_ref[i].astype(F32) for i in range(n_batch * n_ctx * n_mp))
        for i in range(4):
            out_ref[i // 2 : i // 2 + 1, (i % 2) * half : (i % 2 + 1) * half] = terms[i : i + 1, :]

        def total(batch, places, at, size):
            whos = [(batch * n_ctx + place) * n_mp + core for place in places for core in range(n_mp)]
            return sum(in_ref[who].astype(F32)[at : at + 1, :size] for who in whos)

        for group in range(n_ctx):
            size, lane = owned(spans, group, n_heads)
            if not size:
                continue
            value = sum(total(batch, (group,), 6, 2 * width) for batch in range(n_batch))
            out_ref[2:3, lane : lane + size] = value[:, :size]
            out_ref[3:4, lane : lane + size] = value[:, width : width + size]
        early = []
        for i in range(n_batch * n_ctx):
            batch, place = i // n_ctx, i % n_ctx
            early.append(total(batch, (place % top, place % top + top), 4 + place // top, slice_size))
        for i in range(4 * across):
            to = (i % across) * slice_size
            out_ref[4 + i // across : 5 + i // across, to : to + slice_size] = early[i]
        for side in range(n_mp):

            @pl.when(mp_ref[0] == side)
            def _():
                for i in range(hid_half // slice_size):
                    at = 4 * across + side * (hid_half // slice_size) + i
                    up_ref[:, i * slice_size : (i + 1) * slice_size] = early[at]

    results = call(kernel, (mp.reshape(1),), (late,), [array((8, dim), F32), array((1, hid_half), F32)])
    return results[0], results[1].reshape(-1)


def scatter_first(keep, got, rows, after=()):
    dim = keep.shape[1]
    half = rows // 2

    def kernel(keep_ref, got_ref, one_ref, two_ref, own_ref, side_ref):
        def some(first, count):
            return keep_ref[first : first + count, :] + got_ref[first : first + count, :].astype(F32)

        one_ref[...] = some(3 * rows, half).astype(LOW)
        two_ref[...] = some(3 * rows + half, half).astype(LOW)
        own_ref[...] = some(0, rows)
        side_ref[0] = some(rows, rows)
        side_ref[1] = some(2 * rows, rows)

    outs = [array((half, dim)), array((half, dim)), array((rows, dim), F32), array((2, rows, dim), F32)]
    return call(kernel, (), (keep, got), outs, after=after, near=(0, 2, 3, 5))


def scatter_second(side, one, two, after=()):
    _, rows, dim = side.shape
    half = rows // 2

    def kernel(side_ref, one_ref, two_ref, batch_ref, near_ref):
        batch_ref[:half, :] = (side_ref[0, :half, :] + one_ref[...].astype(F32)).astype(LOW)
        batch_ref[half:, :] = side_ref[0, half:, :].astype(LOW)
        near_ref[:half, :] = side_ref[1, :half, :].astype(LOW)
        near_ref[half:, :] = (side_ref[1, half:, :] + two_ref[...].astype(F32)).astype(LOW)

    outs = [array((rows, dim)), array((rows, dim))]
    return call(kernel, (), (side, one, two), outs, after=after, near=(0, 3, 4))


def finish_out(mid, acc, one, two, bias, after=()):
    rows, dim = mid.shape

    def kernel(mid_ref, acc_ref, one_ref, two_ref, bias_ref, out_ref):
        own = acc_ref[...] + one_ref[...].astype(F32) + two_ref[...].astype(F32)
        out_ref[0] = (mid_ref[...] + own + row(bias_ref[...])).T.astype(LOW)

    return call(kernel, (), (mid, acc, one, two, bias), [array((1, dim, rows))], after=after)[0]


def back_out(mp, spans, width, summed, mid, cot, gain, weight):
    acc, one, two = summed
    rows, dim = mid.shape
    n = len(spans)
    cols = dim // 2
    steps = 1
    chunk = dim // steps

    def kernel(mp_ref, acc_ref, one_ref, two_ref, mid_ref, cot_ref, gain_ref, w_ref, *refs):
        _, keep_ref, away_ref, _, outs_ref, low_ref, turned_ref = refs
        step = pl.program_id(0)
        pl.when(step == 0)(functools.partial(first, acc_ref, one_ref, two_ref, mid_ref, cot_ref, gain_ref, refs))
        here = pl.ds(pl.multiple_of(step * chunk, 8), chunk)
        turned_ref[here, :] = dot(w_ref[...], low_ref[...], ((1,), (1,)))

        @pl.when(step == steps - 1)
        def _():
            for group in range(n):
                start = spans[group] * HD
                outs_ref[group] = turned_ref[start : start + width, :].T.astype(LOW)
            for side in range(2):

                @pl.when(mp_ref[0] == side)
                def _():
                    keep_ref[...] = low_ref[:, side * cols : (side + 1) * cols]
                    away_ref[...] = low_ref[:, (1 - side) * cols : (2 - side) * cols]

    def first(acc_ref, one_ref, two_ref, mid_ref, cot_ref, gain_ref, refs):
        grad_ref, _, _, sums_ref, _, low_ref, _ = refs
        full = acc_ref[...] + one_ref[...].astype(F32) + two_ref[...].astype(F32)
        xhat, rstd = norm_parts(mid_ref[...])
        back, gain_grad, shift_grad = norm_back(full, xhat, rstd, row(gain_ref[...]))
        cot_full = cot_ref[0].astype(F32)
        grad = cot_full + back
        grad_ref[...] = grad
        low_ref[...] = grad.astype(LOW)
        sums_ref[0:1, :] = jnp.sum(grad, axis=0, keepdims=True)
        sums_ref[1:2, :] = row(gain_grad)
        sums_ref[2:3, :] = row(shift_grad)
        sums_ref[3:4, :] = jnp.sum(cot_full, axis=0, keepdims=True)

    return call(
        kernel,
        (mp.reshape(1),),
        (acc, one, two, mid, cot, gain, weight),
        [
            array((rows, dim), F32),
            array((rows, cols)),
            array((rows, cols)),
            array((4, dim), F32),
            array((n, rows, width)),
        ],
        scratch=[pltpu.VMEM((rows, dim), LOW), pltpu.VMEM((dim, rows), F32)],
        grid=(steps,),
        in_specs=[None] * 6 + [tall(chunk, dim)],
        flops=2 * rows * dim * dim,
    )


def back_qkv(ctx, spans, pieces, weight, tokens, gain, grad_mid, after=()):
    rows, dim = tokens.shape[1:]
    n = len(spans)
    n_heads = dim // HD
    width = pieces[0].shape[1] // 3
    steps = 5 if dim % 40 == 0 else 1
    chunk = dim // steps

    def kernel(ctx_ref, *refs):
        w_ref, x_ref, gain_ref, mid_ref, out_ref, vec_ref, in_ref, all_ref, part_ref = refs[n:]
        step = pl.program_id(0)

        @pl.when(step == 0)
        def _():
            for other in range(n):
                in_ref[ctx_ref[0] ^ other] = refs[other][...]
            for group in range(n):
                size, lane = owned(spans, group, n_heads)
                for part in range(3 if size else 0):
                    to = part * dim + lane
                    all_ref[:, to : to + size] = in_ref[group, :, part * width : part * width + size]

        part_ref[pl.ds(pl.multiple_of(step * chunk, 8), chunk), :] = dot(w_ref[...], all_ref[...], ((1,), (1,)))

        @pl.when(step == steps - 1)
        def _():
            xhat, rstd = norm_parts(x_ref[0].astype(F32))
            back, gain_grad, shift_grad = norm_back(part_ref[...].T, xhat, rstd, row(gain_ref[...]))
            out_ref[0] = (mid_ref[...] + back).T.astype(LOW)
            vec_ref[0:1, :] = row(gain_grad)
            vec_ref[1:2, :] = row(shift_grad)

    in_specs = [None] * n + [tall(chunk, 3 * dim), None, None, None]
    return call(
        kernel,
        (ctx.reshape(1),),
        (*pieces, weight, tokens, gain, grad_mid),
        [array((1, dim, rows)), array((2, dim), F32)],
        scratch=[
            pltpu.VMEM((n, rows, 3 * width), LOW),
            pltpu.VMEM((rows, 3 * dim), LOW),
            pltpu.VMEM((dim, rows), F32),
        ],
        grid=(steps,),
        in_specs=in_specs,
        flops=6 * rows * dim * dim,
        after=after,
    )


def layer(
    tokens, cotangent, block_table, w_qkv, q_bias, v_bias, w_out, out_bias,
    ln1_gain, ln1_bias, ln2_gain, ln2_bias, w_up, up_bias, w_down, down_bias,
):
    n_ctx, n_mp, n_batch = lax.axis_size(CTX), lax.axis_size(MP), lax.axis_size(BATCH)
    ctx, mp, batch = lax.axis_index(CTX), lax.axis_index(MP), lax.axis_index(BATCH)
    rows, dim = tokens.shape[1], tokens.shape[2]
    total = rows * n_ctx
    SENT.clear()
    KEPT.clear()
    GRANT[0] = (36 if total <= 1024 else 60) << 20
    blk = total // block_table.shape[0]
    n_heads = dim // HD
    per = -(-n_heads // n_ctx)
    width = per * HD
    hid_half = w_up.shape[1]
    near = (ctx // NEAR) % 2
    member = batch * 2 + near
    hid = hid_half // (2 * n_batch)
    part = dim // (n_batch * n_ctx)
    half = rows // 2
    spans = [group * (n_heads - per) // (n_ctx - 1) for group in range(n_ctx)]

    ring = ring_of(n_ctx)
    place = [ring.index(i) for i in range(n_ctx)]
    ring_arr = jnp.array(ring, jnp.int32)
    at = jnp.array(place, jnp.int32)[ctx]
    steps = jnp.arange(n_ctx, dtype=jnp.int32)
    ranks = (at - jnp.array(place, jnp.int32)) % n_ctx
    sources = ring_arr[(at - steps) % n_ctx]
    blocks_per = rows // blk
    order = block_table.reshape(n_ctx, blocks_per)[sources].reshape(-1)

    starts_of = jnp.array(spans, jnp.int32) * HD
    head_start = starts_of[ctx]
    w_own = jnp.concatenate(
        [lax.dynamic_slice(w_qkv, (0, head_start + i * dim), (dim, width)) for i in range(3)], axis=1
    )
    bias_own = jnp.concatenate(
        [
            lax.dynamic_slice(q_bias, (head_start,), (width,)),
            jnp.zeros((width,), F32),
            lax.dynamic_slice(v_bias, (head_start,), (width,)),
        ]
    )

    def gather_first(own, own_near, far):
        return flip(own, BATCH, 1, far), flip(own_near, CTX, NEAR, far)

    def gather_second(sides, far):
        return flip(sides[0][:half], CTX, NEAR, far), flip(sides[1][half:], BATCH, 1, far)

    def exchange(blocks):
        return sent(lax.all_to_all(blocks, CTX, split_axis=0, concat_axis=0, tiled=True))

    tokens, normed_one = norm_in(tokens.transpose(0, 2, 1), ln1_gain, ln1_bias)
    normed_pieces = ring_gather(normed_one, ring)
    w_down_own = lax.dynamic_slice(w_down.T, (0, member * hid), (dim, hid))
    up_bias_own = lax.dynamic_slice(up_bias, (member * hid,), (hid,))
    qkv, normed_all = project_qkv(order, normed_pieces, w_own, row(bias_own), blk, (w_down_own, up_bias_own))

    cot_own = cotangent[0]
    cot_near, _ = lax.optimization_barrier((cot_own, normed_pieces[n_ctx // 2]))
    cot_sides = gather_first(cot_own, cot_near, True)
    attn_heads, lse = attn_forward(order, sources, qkv, rows, blk)
    attn_pieces = exchange(attn_heads)
    cot_chip = pack([cot_own, *cot_sides, *gather_second(cot_sides, True)], (lse,))
    cot_groups = cot_chip, flip(cot_chip, MP, 1)
    attn_rows, resid_mid, normed_two = project_out(
        spans, attn_pieces, w_out, tokens, (out_bias, ln2_gain, ln2_bias), (cot_chip,)
    )

    near_rows = gather_first(normed_two, normed_two, False)
    far_rows = gather_second(near_rows, False)
    w_up_later, _ = lax.optimization_barrier((w_up, normed_two))
    w_up_own = lax.dynamic_slice(w_up_later, (0, member * hid), (dim, hid))
    hidden_back_keep = feed_dot(cot_groups[0], w_down_own, False, F32, (normed_two,))
    normed_chip = pack([normed_two, *near_rows, *far_rows], (hidden_back_keep,))
    normed_groups = normed_chip, flip(normed_chip, MP, 1)
    hidden_back_away = feed_dot(cot_groups[1], w_down_own, False, F32, (normed_chip,), (1, 2))
    hidden_away, low_away, back_away, sum_away = feed(
        normed_groups[1], w_up_own, up_bias_own, hidden_back_away, LOW, (), (1, 3, 6)
    )
    hidden_keep, low_keep, back_keep, sum_keep = feed(
        normed_groups[0], w_up_own, up_bias_own, hidden_back_keep, F32, (back_away,), (1, 6)
    )
    one, two, acc, side = scatter_first(back_keep, flip(back_away, MP, 1), rows)
    one_got, two_got = flip(one, CTX, NEAR), flip(two, BATCH, 1)
    by_batch, by_near = scatter_second(side, one_got, two_got)
    down_away = feed_dot(hidden_away, w_down_own, True, LOW, (by_near,))
    grad_normed_two = acc, flip(by_batch, BATCH, 1), flip(by_near, CTX, NEAR)
    up_shift_grad = (sum_keep + sum_away).reshape(-1)

    grad_mid, mid_keep, mid_away, mid_vectors, by_group = back_out(
        mp, spans, width, grad_normed_two, resid_mid, cotangent, ln2_gain, w_out
    )
    grad_heads = exchange(by_group)

    bits = []
    bit = 1
    while bit < n_ctx:
        bits.append(bit)
        bit *= 2

    def feed_grad(lefts, rights, after):
        away, keep = weight_grad(ctx % 2, lefts, rights, part, (n_batch * n_ctx // 2, 1), after)
        return flip(away, CTX, 1), keep

    def feed_half(got, keep, after=()):
        left = [bit for bit in reversed(bits) if bit > 1]
        halves = [bit for bit in bits if bit > 1 and bit != NEAR]
        first = None
        for bit in halves:
            lead = n_batch * 2 ** left.index(bit)
            tail = 2 ** (len(left) - 1 - left.index(bit))
            away, keep = halve((ctx // bit) % 2, keep, got, (lead, tail), after if first is None else ())
            first = away if first is None else first
            got = flip(away, CTX, bit)
            left.remove(bit)
        return first, got, keep

    def feed_swap(got, keep, after=()):
        mine, to_batch, to_near, to_both = swap_blocks(member, keep, got, after)
        pairs = [(b * n_ctx + c, (1 - b) * n_ctx + (c ^ NEAR)) for b in range(n_batch) for c in range(n_ctx)]
        both = permute(to_both, (BATCH, CTX), pairs)
        far, got = flip(to_batch, BATCH, 1), flip(to_near, CTX, NEAR)
        return mine, (mine, far, got, both)

    down_got, down_kept = feed_grad(cot_groups, (hidden_keep, hidden_away), (one,))


    everyone = (BATCH, CTX, MP)
    n_all = n_batch * n_ctx * n_mp
    early = jnp.concatenate(
        [
            mid_vectors.reshape(-1),
            lax.dynamic_update_slice(
                jnp.zeros((hid_half * n_mp,), F32), up_shift_grad, (mp * hid_half + member * hid,)
            ),
        ]
    ).reshape(n_batch * n_ctx, -1)
    out_away, out_kept = weight_grad(
        batch, (attn_rows, flip(attn_rows, MP)), (mid_keep, flip(mid_away, MP)), part, (1, n_ctx), (grad_mid,), early
    )
    out_got = flip(out_away, BATCH, 1)
    down_first, down_got, down_kept = feed_half(down_got, down_kept, (out_kept,))
    up_got, up_kept = feed_grad(normed_groups, (low_keep, low_away), (down_first,))
    out_bits = [NEAR] + [bit for bit in bits if bit != NEAR]
    left = bits[::-1]

    def out_half(level, out_got, out_kept, after=(), extra=0):
        bit = out_bits[level]
        lead, tail = 2 ** left.index(bit), 2 ** (len(left) - 1 - left.index(bit))
        left.remove(bit)
        away, keep, *rest = halve((ctx // bit) % 2, out_kept, out_got, (lead, tail), after, part, extra)
        return (away, flip(away, CTX, bit), keep, *rest)


    grad_blocks = attn_backward(order, sources, ranks, ctx, qkv, grad_heads, attn_heads, lse, rows, blk, (up_kept,))
    pieces_back = [grad_blocks[0]] + [flip(grad_blocks[i], CTX, i) for i in range(1, n_ctx)]


    qkv_away, qkv_kept, column_sums = qkv_grad(mp, ranks, ctx, normed_all, grad_blocks, part)
    qkv_got = flip(qkv_away, MP, 1)
    out_first, out_got, out_kept = out_half(0, out_got, out_kept, (qkv_kept,))
    qkv_away, qkv_kept = halve(batch, qkv_kept, qkv_got, (1, n_ctx), (out_first,))
    qkv_got = flip(qkv_away, BATCH, 1)
    up_first, up_got, up_kept = feed_half(up_got, up_kept, (qkv_kept,))

    down_keep = feed_dot(hidden_keep, w_down_own, True, F32, (up_first,), (1, 2))
    last, other, last_acc, last_side = scatter_first(down_keep, flip(down_away, MP), rows)
    last_got, other_got = flip(last, CTX, NEAR), flip(other, BATCH, 1)
    down_swap, down_parts = feed_swap(down_got, down_kept, (last,))
    values = add_blocks(ctx, qkv_kept, qkv_got, (down_swap,))
    received = [values[0]] + [flip(values[i], CTX, i) for i in range(1, n_ctx)]
    for level in range(1, len(bits) - 1):
        out_first, out_got, out_kept = out_half(level, out_got, out_kept, (values[0],))
    tokens_grad_rows, in_vectors = back_qkv(
        ctx, spans, pieces_back, w_qkv, tokens, ln1_gain, grad_mid, (out_first,)
    )
    out_first, out_got, out_kept, early_sum = out_half(
        len(bits) - 1, out_got, out_kept, (in_vectors,), early.shape[1]
    )
    late = pack_late(in_vectors, column_sums, early_sum, n_all, width)
    packed = late
    late = lax.all_to_all(late, everyone, split_axis=0, concat_axis=0, tiled=True)
    vector_sum, up_bias_grad = finish_vectors(
        mp, late, (n_batch, n_ctx, n_mp), spans, dim, hid_half, width, early.shape[1]
    )
    up_swap, up_parts = feed_swap(up_got, up_kept, (packed,))
    last_batch, last_near = scatter_second(last_side, last_got, other_got, (up_swap,))
    last_sides = flip(last_batch, BATCH, 1), flip(last_near, CTX, NEAR)
    down_part = join_feed(member, down_parts, part, (last_near,))
    qkv_part = join_qkv(mp, ctx, spans, received, dim, part, (down_part,))
    out_value = join_out(out_kept, out_got, part, (qkv_part,))
    up_part = join_feed(member, up_parts, part, (out_value,))
    layer_rows = finish_out(resid_mid, last_acc, *last_sides, down_bias, (up_part,))
    down_part = down_part.T
    return (
        layer_rows.transpose(0, 2, 1),
        tokens_grad_rows.transpose(0, 2, 1),
        qkv_part,
        out_value,
        up_part,
        down_part,
        up_bias_grad,
        vector_sum,
    )


def solution(mesh):
    return jax.shard_map(
        layer,
        mesh=mesh,
        in_specs=(
            P((BATCH, MP), CTX, None),
            P((BATCH, MP), CTX, None),
            P(),
            P(),
            P(),
            P(),
            P(),
            P(),
            P(),
            P(),
            P(),
            P(),
            P(None, MP),
            P(MP),
            P(MP, None),
            P(),
        ),
        out_specs=(
            P((BATCH, MP), CTX, None),
            P((BATCH, MP), CTX, None),
            P((BATCH, CTX), MP),
            P((BATCH, CTX), MP),
            P((BATCH, CTX), MP),
            P(MP, (BATCH, CTX)),
            P(MP),
            P(),
        ),
        check_vma=False,
    )
```
